32 devices in a mesh: site: 8 (over z, x), real: 4 (over y, core).
Axes of the slice: x: 2, y: 2, z: 4, core: 2. Of those that a mesh axis runs over, the one named last changes fastest.
Arguments:
- epsilon: bfloat16 [8192, 2048], P('site', 'real'), may hold values from -6 to 6
- factor: bfloat16 [2, 72, 512, 512], P(None, 'site'), may hold values from -0.09375 to 0.09375
- block_rows: int32 [2, 72], P(None, 'site'), may hold values from 0 to 15, as said below
- median_log: float32 [8192], P('site'), may hold values from -2.5 to -0.5
- spread_log: float32 [8192], P('site'), may hold values from 0.4 to 0.8
- critical_yield: float32 [8192], P('site'), may hold values from 0.03 to 0.3
Outputs:
- residual_field: bfloat16 [8192, 2048], P('site', 'real')
- mean_damage: float32 [8192], P('site')
The draws below stay inside these ranges and needn't reach their ends.
Inputs may be any that keep to these rules, and one draw needn't show every extreme that they name: block_rows[p, b] = (c + o) mod 16, with c = 2 * (b // 9) + p the block's column tile and o in 0 to 11; the offsets o of one block column are distinct, and the first block of each column has o = 0.
All inputs are finite; a program needn't handle non-finite values.
Results may differ from the reference program's by a relative error of at most 0.001.
Values sent between devices are 32-bit elements; how exact they have to be, the bound alone decides.
A program may use at most 256 MiB of HBM per device.

```python
import math
import jax
import jax.numpy as jnp
from jax import lax

TILE = 512
PANELS = 2
BLOCKS = 9
BAND = 12
TILES = 16
NBLK = 72
SITES = 8192
REALS = 2048


def draw_block_rows(key, part):
    columns = TILES // PANELS
    scores = jax.random.randint(key, (PANELS, columns, BAND - 1), 0, 1 << 20) * BAND
    scores = scores + jnp.arange(BAND - 1, dtype=jnp.int32)
    chosen = jnp.argsort(scores, axis=-1)[:, :, :BLOCKS - 1].astype(jnp.int32) + 1
    offsets = jnp.concatenate([jnp.zeros((PANELS, columns, 1), jnp.int32), chosen], axis=-1)
    column_tile = PANELS * jnp.arange(columns, dtype=jnp.int32)[None, :, None] + jnp.arange(PANELS, dtype=jnp.int32)[:, None, None]
    result = (column_tile + offsets) % TILES
    return result.reshape(PANELS, columns * BLOCKS).astype(jnp.int32)


def levels(rng, shape, pieces, least, high):
    level = 1.0
    for position, blocks in pieces:
        steps = jax.random.uniform(jax.random.fold_in(jax.random.fold_in(rng, 6), position), (blocks,), jnp.float32, least / len(pieces), high / len(pieces))
        level = level * jnp.repeat(jnp.exp(steps), shape[position] // blocks).reshape((-1,) + (1,) * (len(shape) - 1 - position))
    return level


def centred(own_key, extent, spread, most, cuts=(), kind=jnp.bfloat16):
    gain = levels(own_key, extent, cuts, -0.22, 0.18) if cuts else 1.0
    drawn = jax.random.normal(own_key, extent, jnp.float32) * spread * gain
    return jnp.minimum(jnp.maximum(drawn, -most), most).astype(kind)


def setup_inputs(seed: int = 0) -> dict:
    streams_of = jax.random.split(jax.random.key(seed), 7)
    return {
        "epsilon": centred(streams_of[0], (SITES, REALS), 1.0, 6.0, ((0, 8), (1, 4))),
        "factor": centred(streams_of[1], (PANELS, NBLK, TILE, TILE), (TILE * BLOCKS) ** -0.5, 0.09375, ((1, 8),)),
        "block_rows": draw_block_rows(jax.random.fold_in(streams_of[6], 71), 0),
        "median_log": jnp.clip(-2.5 + 2.0 * jax.random.uniform(streams_of[3], (SITES,), jnp.float32) ** levels(streams_of[3], (SITES,), ((0, 8),), -0.2, 0.2), -2.5, -0.5),
        "spread_log": jnp.clip(0.4 + 0.4 * jax.random.uniform(streams_of[4], (SITES,), jnp.float32) ** levels(streams_of[4], (SITES,), ((0, 8),), -0.2, 0.2), 0.4, 0.8),
        "critical_yield": jnp.clip(jnp.exp(math.log(0.3) - 2.3025852 * jax.random.uniform(streams_of[5], (SITES,), jnp.float32) ** levels(streams_of[5], (SITES,), ((0, 8),), -0.2, 0.2)), 0.03, 0.3),
    }


coeff_disp = 10.0 ** 0.215
power_margin = 2.341
power_ratio = 1.438


def reference(epsilon, factor, block_rows, median_log, spread_log, critical_yield):
    tiles = SITES // TILE
    draws = epsilon.reshape(tiles, TILE, REALS)
    field = jnp.zeros((tiles, TILE, REALS), jnp.float32)
    for panel in range(PANELS):
        def add_block(carry, item):
            block, target, number = item
            column = (PANELS * (number // BLOCKS) + panel).astype(jnp.int32)
            source = lax.dynamic_index_in_dim(draws, column, 0, keepdims=False)
            product = jnp.dot(block, source, preferred_element_type=jnp.float32)
            return carry.at[target].add(product), None
        numbers = jnp.arange(NBLK, dtype=jnp.int32)
        field, unused = lax.scan(add_block, field, (factor[panel], block_rows[panel], numbers))
    residual_field = field.astype(jnp.bfloat16).reshape(SITES, REALS)
    log_peak = median_log[:, None] + spread_log[:, None] * residual_field.astype(jnp.float32)
    log_ratio = jnp.log(critical_yield)[:, None] - log_peak
    ratio = jnp.exp(log_ratio)
    margin = jnp.maximum(1.0 - ratio, 0.0)
    displacement = coeff_disp * jnp.power(margin, power_margin) * jnp.exp(-power_ratio * log_ratio)
    mean_damage = jnp.sum(jnp.log1p(displacement), axis=1) / REALS
    return residual_field, mean_damage
```

```python
import functools
import jax
import jax.numpy as jnp
from jax import lax
from jax.experimental import pallas as pl
from jax.experimental.pallas import tpu as pltpu
from jax.sharding import PartitionSpec as P

BAND = 12
PAIR = 2
LANES = 128
ROWS = 64
PARTS = 4
HEAD = 2
SITE_TILES = 16
LAST_OFFSET = 12
CROSS, UP, DOWN, KEEP = range(4)
MESH = pl.DeviceIdType.MESH

coeff_disp = 10.0**0.215
power_margin = 2.341
power_ratio = 1.438


def passed_along(value, axis, steps):
    count = lax.axis_size(axis)
    pairs = [(source, (source + steps) % count) for source in range(count)]
    return lax.ppermute(value, axis, pairs)


def shards(epsilon, factor, block_rows, median_log, spread_log, critical_yield):
    panels = factor.shape[0]
    per_column = factor.shape[1]
    tile_size = factor.shape[-1]
    own_reals = epsilon.shape[1]
    reach = BAND // 2
    own_index = lax.axis_index("site")
    total_tiles = panels * lax.axis_size("site")
    draws = epsilon.reshape(panels, tile_size, own_reals)

    def pending(panel):
        flat = factor[panel].reshape(per_column * tile_size, tile_size)
        products = jnp.dot(flat, draws[panel], preferred_element_type=jnp.float32)
        products = products.reshape(per_column, tile_size, own_reals)
        relative = (block_rows[panel] - own_index * panels) % total_tiles
        slots = jnp.zeros(((reach + 1) * panels, tile_size, own_reals), jnp.float32)
        sums = slots.at[relative].set(products, unique_indices=True)
        return sums.reshape(reach + 1, panels, tile_size, own_reals)

    combined = pending(0)
    panel = 1
    combined = combined + pending(panel)
    arrived = combined[0]
    for offset in range(1, reach + 1):
        arrived = arrived + passed_along(combined[offset], "site", offset)
    residual_field = arrived.astype(jnp.bfloat16).reshape(panels * tile_size, own_reals)
    log_peak = median_log[:, None] + spread_log[:, None] * residual_field.astype(jnp.float32)
    log_ratio = jnp.log(critical_yield)[:, None] - log_peak
    ratio = jnp.exp(log_ratio)
    margin = jnp.maximum(1.0 - ratio, 0.0)
    displacement = coeff_disp * jnp.power(margin, power_margin) * jnp.exp(-power_ratio * log_ratio)
    local_total = jnp.sum(jnp.log1p(displacement), axis=1)
    total = lax.psum(local_total, "real")
    mean_damage = total / (own_reals * lax.axis_size("real"))
    return (residual_field, mean_damage)

LEFT, RIGHT, BOTH = (0,), (1,), (0, 1)
ROUTES = {
    0: [({}, {3: LEFT, 2: BOTH, 1: LEFT})] * 2,
    1: [({}, {3: LEFT, 2: BOTH, 1: LEFT})] * 2,
    2: [({}, {3: RIGHT, 2: RIGHT, 1: RIGHT})] * 2,
    3: [({}, {3: RIGHT, 2: RIGHT, 1: RIGHT})] * 2,
    4: [({0: LEFT}, {3: LEFT, 2: LEFT})] * 2,
    5: [({0: LEFT}, {3: LEFT, 2: LEFT})] * 2,
    6: [({0: RIGHT}, {3: RIGHT, 2: RIGHT})] * 2,
    7: [({0: LEFT}, {3: LEFT, 2: LEFT}), ({0: RIGHT}, {3: RIGHT, 2: RIGHT})],
    8: [({0: LEFT, 1: LEFT}, {3: LEFT})] * 2,
    9: [({0: LEFT, 1: BOTH}, {3: RIGHT})] * 2,
    10: [({0: RIGHT, 1: RIGHT}, {3: RIGHT})] * 2,
    11: [({0: RIGHT, 1: RIGHT}, {})] * 2,
    12: [({0: LEFT, 1: LEFT, 2: LEFT}, {})] * 2,
    13: [({0: RIGHT, 1: LEFT, 2: LEFT}, {})] * 2,
    14: [({0: RIGHT, 1: RIGHT, 2: RIGHT}, {})] * 2,
    15: [({1: BOTH, 2: BOTH}, {})] * 2,
}

PLAN = {
    (0, 0): (
        (1, [4, 6, 13, 22, 15, 20, 21, 5, -1, 23, 12, -1, 7]),
        (7, [9, 24, 8, 25, 18, 10, -1, -1, 19, 16, 14, 17, 11]),
        (0, []),
        (23, [1, -1, -1, -1, -1, -1, 2, 3, 0]),
    ),
    (0, 1): (
        (3, [9, 24, 8, 25, 18, 10, -1, 19, 16, 14, 17, 11]),
        (4, [29, 27, 28, 26, 22, -1, 20, 21, 15, 23, 13, 12]),
        (0, []),
        (27, [4, -1, -1, -1, -1, 6, 5, -1, 7]),
    ),
    (1, 0): (
        (4, [13, 23, 29, 28, 21, 22, 12, 15, 20, -1, -1, 14]),
        (10, [31, 30, 27, 24, 18, 25, 26, 19, 16, -1, 17]),
        (16, [1, -1, -1, -1, -1, -1, 2, 3, 0]),
        (38, [9, 8, -1, -1, 10, 11]),
    ),
    (1, 1): (
        (4, [24, 1, 27, 2, 25, 26, 3, 16, 0, 17]),
        (3, [18, 19, 31, 29, -1, 22, 30, 28, 21, 20, 23]),
        (20, [4, -1, 5, -1, 7, 6]),
        (39, [15, 14, 13, 12]),
    ),
    (2, 0): (
        (0, [22, 4, -1, 29, 5, 7, 6, 21, 20, -1, 28, 23]),
        (13, [31, -1, 30, 24, -1, -1, 27, -1, 25, 26]),
        (15, [1, 0, 2, 11, 3, 9, 8, 14, 10]),
        (35, [18, -1, -1, 19, 17, 16]),
    ),
    (2, 1): (
        (3, [9, 8, 11, 24, 25, 18, -1, 27, 10, 26, -1, 19]),
        (16, [31, -1, 29, -1, -1, -1, 30, 28]),
        (0, [1, 0, 3, -1, 2, 4, 5, 6, -1, 15, 7, 12, 13]),
        (43, [22, 21, 20, 23]),
    ),
    (3, 0): (
        (0, [4, -1, -1, 15, 6, 5, 31, 12, 7, 30, 13, 28, 29]),
        (0, []),
        (10, [11, 1, 0, 2, 8, 3, 9, 14, 10, 17, 16]),
        (31, [24, -1, -1, -1, 27, 25, 26]),
    ),
    (3, 1): (
        (3, [11, -1, 1, -1, 0, 2, 8, 3, 9, 14, 10, 17, 16]),
        (0, []),
        (8, [18, 4, -1, 15, 6, 5, 19, 12, 7, 21, 13, 20]),
        (34, [31, -1, -1, -1, 30, 29, 28]),
    ),
}


def device_steps(depth, panels):
    steps = {(z, x): {} for z in range(depth) for x in range(PAIR)}

    def plane(z, unit, leaves, onward, arriving):
        own = [(unit // 2 - panels * (PAIR * z + x)) % SITE_TILES <= LAST_OFFSET for x in range(PAIR)]
        held = [x for x in range(PAIR) if own[x] or arriving.get(x)]
        for x in held:
            if x not in leaves:
                steps[z, x][unit] = (own[x], tuple(arriving.get(x, ())), CROSS)
        crossed = (CROSS,) if any(x not in leaves for x in held) else ()
        for x in leaves:
            steps[z, x][unit] = (own[x], tuple(arriving.get(x, ())) + crossed, onward)

    for row, halves in ROUTES.items():
        home, column = row // (panels * PAIR), row // panels % PAIR
        for half, (rising, falling) in enumerate(halves):
            unit, merged = 2 * row + half, {}
            for onward, path, planes in ((UP, rising, range(home)), (DOWN, falling, range(depth - 1, home, -1))):
                arriving = {}
                for z in planes:
                    if z in path:
                        plane(z, unit, path[z], onward, arriving)
                        arriving = {x: (onward,) for x in path[z]}
                for x, kinds in arriving.items():
                    merged[x] = merged.get(x, ()) + kinds
            plane(home, unit, (column,), KEEP, merged)
    return steps


def stream_words(depth, panels):
    steps = device_steps(depth, panels)

    def target(device, way):
        z, x = device
        return {CROSS: (z, 1 - x), UP: (z + 1, x), DOWN: (z - 1, x)}[way]

    bases = {}
    for device, streams in PLAN.items():
        for way in (CROSS, UP, DOWN):
            sent = [unit for unit in streams[way][1] if unit >= 0]
            assert all(steps[device][unit][2] == way for unit in sent)
            for base, unit in enumerate(sent):
                bases[target(device, way), unit, way] = base
    words = {}
    for device, streams in PLAN.items():
        planned = [unit for stream in streams for unit in stream[1] if unit >= 0]
        assert sorted(planned) == sorted(steps[device])
        first, words[device] = panels * (PAIR * device[0] + device[1]), []
        for way, (start, units) in enumerate(streams):
            line = []
            for unit in units:
                if unit < 0:
                    line.append(0)
                    continue
                own, arriving, onward = steps[device][unit]
                assert onward == way
                base = 0 if way == KEEP else bases[target(device, way), unit, way]
                word = 1 + 2 * ((unit - 2 * first) % (2 * SITE_TILES)) + 64 * base
                for kind in arriving:
                    word += (1 + 2 * bases[device, unit, kind]) * 1024 * 32**kind
                line.append(word)
            words[device].append((start, line))
        own, arriving, _ = steps[device][streams[CROSS][1][0]]
        assert own and not arriving
    return words


def field_kernel(
    words, own_reals, block_rows, eps_in, factor_in, median, spread, critical, field_out, mean_out,
    eps, factor, head, x_out, u_out, d_out, x_in, u_in, d_in, spare, totals, columns, folds, table, field,
    load_sem, x_send, u_send, d_send, x_recv, u_recv, d_recv, t_send, t_recv, f_send,
):
    panels, per_column, tile = factor.shape[0], factor.shape[1], factor.shape[2]
    depth = len(words) // PAIR
    count = PAIR * depth
    chunks = panels * tile // ROWS
    per_tile = tile // ROWS
    per_unit = per_tile // 2
    lines = panels * tile // LANES
    reals = lax.axis_size("real")
    site = lax.axis_index("site")
    me = lax.axis_index("real")
    z, x = site // PAIR, site % PAIR
    here = {device: site == device[0] * PAIR + device[1] for device in words}

    def pick(values):
        result = None
        for device, value in values.items():
            value = jnp.int32(value)
            result = value if result is None else jnp.where(here[device], value, result)
        return result

    begin = pick({
        device: (own[CROSS][1][0] // 2 % 2) * (tile // 2) for device, own in words.items()
    })
    first = [pltpu.make_async_copy(eps_in, eps, load_sem.at[0])]
    rest = []
    for panel in range(panels):
        first.append(pltpu.make_async_copy(
            factor_in.at[panel, :, pl.ds(pl.multiple_of(begin, tile // 2), head.shape[2]), :],
            head.at[panel], load_sem.at[1 + panel],
        ))
        rest.append(pltpu.make_async_copy(
            factor_in.at[panel], factor.at[panel], load_sem.at[1 + panels + panel]
        ))
    for load in first + rest:
        load.start()

    barrier = pltpu.get_barrier_semaphore()
    pl.semaphore_signal(barrier, inc=1, device_id={"site": site + 1 - 2 * x}, device_id_type=MESH)
    for shift in range(1, reals):
        pl.semaphore_signal(barrier, inc=1, device_id={"real": (me + shift) % reals}, device_id_type=MESH)

    @pl.when(z > 0)
    def _():
        pl.semaphore_signal(barrier, inc=1, device_id={"site": site - PAIR}, device_id_type=MESH)

    @pl.when(z < depth - 1)
    def _():
        pl.semaphore_signal(barrier, inc=1, device_id={"site": site + PAIR}, device_id_type=MESH)

    plan, starts, sent, slots = [], [], [], 0
    for way in range(4):
        longest = max(len(own[way][1]) for own in words.values())
        plan.append([
            pick({device: (own[way][1] + [0] * longest)[number] for device, own in words.items()})
            for number in range(longest)
        ])
        starts.append(pick({device: own[way][0] for device, own in words.items()}))
        sent.append(pick({
            device: per_unit * sum(word > 0 for word in own[way][1]) for device, own in words.items()
        }))
        slots = max([slots] + [own[way][0] + per_unit * len(own[way][1]) for own in words.values()])

    for panel in range(panels):
        begins = [
            (block_rows[panel, block] - site * panels + panels * count) % (panels * count)
            for block in range(per_column)
        ]

        @pl.loop(0, table.shape[1])
        def _(slot):
            number, found = jnp.int32(0), jnp.int32(0)
            for block in range(per_column):
                hit = begins[block] == slot
                number = jnp.where(hit, block, number)
                found = jnp.where(hit, 1, found)
            table[panel, slot] = number
            table[panels + panel, slot] = found

    pl.semaphore_wait(barrier, reals + jnp.where(z > 0, 1, 0) + jnp.where(z < depth - 1, 1, 0))

    for load in first:
        load.wait()

    def bits(word, low, width):
        return lax.rem(lax.div(word, jnp.int32(2**low)), jnp.int32(2**width))

    def multiply(out, relative, piece, source):
        @pl.when(relative <= LAST_OFFSET)
        def _():
            row = pl.multiple_of(piece * ROWS, ROWS)
            result = None
            for panel in range(panels):
                block = source[panel, table[panel, relative], pl.ds(row, ROWS), :]
                product = jnp.dot(
                    block, eps[panel * tile:(panel + 1) * tile, :], preferred_element_type=jnp.float32
                ) * table[panels + panel, relative].astype(jnp.float32)
                result = product if result is None else result + product
            out[...] = result

        @pl.when(relative > LAST_OFFSET)
        def _():
            out[...] = jnp.zeros_like(out)

    ways = (
        (x_out, x_in, x_send, x_recv, site + 1 - 2 * x),
        (u_out, u_in, u_send, u_recv, (site + PAIR) % count),
        (d_out, d_in, d_send, d_recv, (site + count - PAIR) % count),
    )

    def copy(way, slot):
        leaving, landing, departure, arrival, there = ways[way]
        return pltpu.make_async_remote_copy(
            src_ref=leaving.at[slot],
            dst_ref=landing.at[slot],
            send_sem=departure.at[slot],
            recv_sem=arrival.at[slot],
            device_id={"site": there},
            device_id_type=MESH,
        )

    def field_copy(chunk):
        rows = pl.ds(pl.multiple_of(chunk * ROWS, ROWS), ROWS)
        return pltpu.make_async_copy(field.at[chunk], field_out.at[rows, :], f_send.at[chunk])

    def keep(chunk):
        rounded = spare[...].astype(jnp.bfloat16)
        rows = pl.ds(pl.multiple_of(chunk * ROWS, ROWS), ROWS)
        field[chunk] = rounded
        field_copy(chunk).start()
        folded = None
        for piece in range(own_reals // LANES):
            residual = rounded[:, piece * LANES:(piece + 1) * LANES].astype(jnp.float32)
            log_peak = columns[0, rows, :] + columns[1, rows, :] * residual
            log_ratio = columns[2, rows, :] - log_peak
            margin = jnp.maximum(1.0 - jnp.exp(log_ratio), 0.0)
            displacement = coeff_disp * jnp.exp(power_margin * jnp.log(margin) - power_ratio * log_ratio)
            damage = jnp.log1p(displacement)
            folded = damage if folded is None else folded + damage
        folds[rows, :] = folded

        @pl.when((chunk + 1) % (LANES // ROWS) == 0)
        def _():
            line = chunk // (LANES // ROWS)
            group = folds[pl.ds(pl.multiple_of(line * LANES, LANES), LANES), :]
            totals[me, pl.ds(line, 1), :] = jnp.sum(group.T, axis=0, keepdims=True)

    def step(way, slot, source, least=0):
        number = slot - starts[way] + per_unit * slots
        group = lax.div(number, jnp.int32(per_unit)) - slots
        turn = lax.rem(number, jnp.int32(per_unit))
        word = jnp.int32(0)
        for index, value in enumerate(plan[way]):
            word = jnp.where(group == index, value, word)

        @pl.when(jnp.logical_and(word > 0, slot - starts[way] >= least))
        def _():
            relative = bits(word, 2, 4)
            piece = bits(word, 1, 1) * per_unit + turn
            place = bits(word, 6, 4) * per_unit + turn
            out = spare if way == KEEP else ways[way][0].at[place]
            multiply(out, relative, piece if source is factor else turn, source)
            if source is not factor:
                copy(way, place).start()
                return
            for kind in range(3):
                @pl.when(bits(word, 10 + 5 * kind, 1) == 1)
                def _():
                    arrived = bits(word, 11 + 5 * kind, 4) * per_unit + turn
                    copy(kind, arrived).wait_recv()
                    out[...] = out[...] + ways[kind][1][arrived]

            if way == KEEP:
                keep(relative * per_tile + piece)
            else:
                copy(way, place).start()

    for slot in range(HEAD):
        step(CROSS, starts[CROSS] + slot, head)
    for load in rest:
        load.wait()

    @pl.loop(0, slots)
    def _(slot):
        step(CROSS, slot, factor, HEAD)

        @pl.when(slot < lines)
        def _():
            spot = pl.ds(pl.multiple_of(slot * LANES, LANES), LANES)
            for index, ref in enumerate((median, spread, critical)):
                value = ref[pl.ds(slot, 1), :]
                value = jnp.log(value) if index == 2 else value
                columns[index, spot, :] = jnp.broadcast_to(value, (LANES, LANES)).T

        for way in (UP, DOWN, KEEP):
            step(way, slot, factor)

    def t_copy(shift):
        return pltpu.make_async_remote_copy(
            src_ref=totals.at[me],
            dst_ref=totals.at[me],
            send_sem=t_send.at[shift],
            recv_sem=t_recv.at[shift],
            device_id={"real": (me + shift) % reals},
            device_id_type=MESH,
        )

    for shift in range(1, reals):
        t_copy(shift).start()

    for way in (CROSS, UP, DOWN):
        @pl.loop(0, sent[way])
        def _(slot):
            copy(way, slot).wait_send()

    @pl.loop(0, chunks)
    def _(chunk):
        field_copy(chunk).wait()

    for shift in range(1, reals):
        t_copy(shift).wait()
    total = totals[0]
    for source in range(1, reals):
        total = total + totals[source]
    mean_out[...] = total / (own_reals * reals)


def hand_out_kernel(field_in, mean_in, field_out, mean_out, field, mean, in_sem, out_sem):
    part = field.shape[1]
    reads = [pltpu.make_async_copy(mean_in, mean, in_sem.at[PARTS])]
    writes = [pltpu.make_async_copy(mean, mean_out, out_sem.at[PARTS])]
    for index in range(PARTS):
        rows = pl.ds(index * part, part)
        reads.append(pltpu.make_async_copy(field_in.at[rows, :], field.at[index], in_sem.at[index]))
        writes.append(pltpu.make_async_copy(field.at[index], field_out.at[rows, :], out_sem.at[index]))
    for read in reads:
        read.start()
    for read, write in zip(reads, writes):
        read.wait()
        write.start()
    for write in writes:
        write.wait()


def line_shards(epsilon, factor, block_rows, median_log, spread_log, critical_yield):
    panels, per_column, tile = factor.shape[:3]
    sites, own_reals = epsilon.shape
    count, reals = lax.axis_size("site"), lax.axis_size("real")
    chunks = sites // ROWS
    lines = sites // LANES
    words = stream_words(count // PAIR, panels)
    most = [
        max(sum(word > 0 for word in own[way][1]) for own in words.values()) * (tile // ROWS // 2)
        for way in (CROSS, UP, DOWN)
    ]
    piece = (ROWS, own_reals)
    vmem = pl.BlockSpec(memory_space=pltpu.VMEM)
    anywhere = pl.BlockSpec(memory_space=pl.ANY)
    field, mean = pl.pallas_call(
        functools.partial(field_kernel, words, own_reals),
        out_shape=(
            jax.ShapeDtypeStruct((sites, own_reals), jnp.bfloat16),
            jax.ShapeDtypeStruct((lines, LANES), jnp.float32),
        ),
        in_specs=[pl.BlockSpec(memory_space=pltpu.SMEM), anywhere, anywhere, vmem, vmem, vmem],
        out_specs=(anywhere, vmem),
        scratch_shapes=[
            pltpu.VMEM(epsilon.shape, epsilon.dtype),
            pltpu.VMEM(factor.shape, factor.dtype),
            pltpu.VMEM((panels, per_column, HEAD * ROWS, tile), factor.dtype),
            *[pltpu.VMEM((slots,) + piece, jnp.float32) for slots in most + most],
            pltpu.VMEM(piece, jnp.float32),
            pltpu.VMEM((reals, lines, LANES), jnp.float32),
            pltpu.VMEM((3, sites, LANES), jnp.float32),
            pltpu.VMEM((sites, LANES), jnp.float32),
            pltpu.SMEM((2 * panels, SITE_TILES), jnp.int32),
            pltpu.VMEM((chunks, ROWS, own_reals), jnp.bfloat16),
            pltpu.SemaphoreType.DMA((1 + 2 * panels,)),
            *[pltpu.SemaphoreType.DMA((slots,)) for slots in most + most],
            pltpu.SemaphoreType.DMA((reals,)),
            pltpu.SemaphoreType.DMA((reals,)),
            pltpu.SemaphoreType.DMA((chunks,)),
        ],
        compiler_params=pltpu.CompilerParams(
            collective_id=0, has_side_effects=True, vmem_limit_bytes=60 * 1024 * 1024
        ),
    )(
        block_rows,
        epsilon,
        factor,
        median_log.reshape(lines, LANES),
        spread_log.reshape(lines, LANES),
        critical_yield.reshape(lines, LANES),
    )
    field, mean = pl.pallas_call(
        hand_out_kernel,
        out_shape=(
            jax.ShapeDtypeStruct(field.shape, field.dtype),
            jax.ShapeDtypeStruct(mean.shape, mean.dtype),
        ),
        in_specs=[anywhere, anywhere],
        out_specs=(anywhere, anywhere),
        scratch_shapes=[
            pltpu.VMEM((PARTS, sites // PARTS, own_reals), field.dtype),
            pltpu.VMEM(mean.shape, mean.dtype),
            pltpu.SemaphoreType.DMA((PARTS + 1,)),
            pltpu.SemaphoreType.DMA((PARTS + 1,)),
        ],
    )(field, mean)
    return field, mean.reshape(sites)


def solution(mesh):
    body = line_shards if mesh.shape["site"] == BAND // 2 + PAIR else shards
    return jax.shard_map(
        body,
        mesh=mesh,
        in_specs=(
            P("site", "real"),
            P(None, "site", None, None),
            P(None, "site"),
            P("site"),
            P("site"),
            P("site"),
        ),
        out_specs=(P("site", "real"), P("site")),
        check_vma=False,
    )
```

```python
import functools
import jax
import jax.numpy as jnp
from jax import lax
from jax.experimental import pallas as pl
from jax.experimental.pallas import tpu as pltpu
from jax.sharding import PartitionSpec as P

BAND = 12
PAIR = 2
LANES = 128
ROWS = 64
PARTS = 4
HEAD = 2
SITE_TILES = 16
LAST_OFFSET = 12
CROSS, UP, DOWN, KEEP = range(4)
MESH = pl.DeviceIdType.MESH

coeff_disp = 10.0**0.215
power_margin = 2.341
power_ratio = 1.438


def passed_along(value, axis, steps):
    count = lax.axis_size(axis)
    pairs = [(source, (source + steps) % count) for source in range(count)]
    return lax.ppermute(value, axis, pairs)


def shards(epsilon, factor, block_rows, median_log, spread_log, critical_yield):
    panels = factor.shape[0]
    per_column = factor.shape[1]
    tile_size = factor.shape[-1]
    own_reals = epsilon.shape[1]
    reach = BAND // 2
    own_index = lax.axis_index("site")
    total_tiles = panels * lax.axis_size("site")
    draws = epsilon.reshape(panels, tile_size, own_reals)

    def pending(panel):
        flat = factor[panel].reshape(per_column * tile_size, tile_size)
        products = jnp.dot(flat, draws[panel], preferred_element_type=jnp.float32)
        products = products.reshape(per_column, tile_size, own_reals)
        relative = (block_rows[panel] - own_index * panels) % total_tiles
        slots = jnp.zeros(((reach + 1) * panels, tile_size, own_reals), jnp.float32)
        sums = slots.at[relative].set(products, unique_indices=True)
        return sums.reshape(reach + 1, panels, tile_size, own_reals)

    combined = pending(0)
    panel = 1
    combined = combined + pending(panel)
    arrived = combined[0]
    for offset in range(1, reach + 1):
        arrived = arrived + passed_along(combined[offset], "site", offset)
    residual_field = arrived.astype(jnp.bfloat16).reshape(panels * tile_size, own_reals)
    log_peak = median_log[:, None] + spread_log[:, None] * residual_field.astype(jnp.float32)
    log_ratio = jnp.log(critical_yield)[:, None] - log_peak
    ratio = jnp.exp(log_ratio)
    margin = jnp.maximum(1.0 - ratio, 0.0)
    displacement = coeff_disp * jnp.power(margin, power_margin) * jnp.exp(-power_ratio * log_ratio)
    local_total = jnp.sum(jnp.log1p(displacement), axis=1)
    total = lax.psum(local_total, "real")
    mean_damage = total / (own_reals * lax.axis_size("real"))
    return (residual_field, mean_damage)

LEFT, RIGHT, BOTH = (0,), (1,), (0, 1)
ROUTES = {
    0: [({}, {3: LEFT, 2: BOTH, 1: LEFT})] * 2,
    1: [({}, {3: LEFT, 2: BOTH, 1: LEFT})] * 2,
    2: [({}, {3: RIGHT, 2: RIGHT, 1: RIGHT})] * 2,
    3: [({}, {3: RIGHT, 2: RIGHT, 1: RIGHT})] * 2,
    4: [({0: LEFT}, {3: LEFT, 2: LEFT})] * 2,
    5: [({0: LEFT}, {3: LEFT, 2: LEFT})] * 2,
    6: [({0: RIGHT}, {3: RIGHT, 2: RIGHT})] * 2,
    7: [({0: LEFT}, {3: LEFT, 2: LEFT}), ({0: RIGHT}, {3: RIGHT, 2: RIGHT})],
    8: [({0: LEFT, 1: LEFT}, {3: LEFT})] * 2,
    9: [({0: LEFT, 1: BOTH}, {3: RIGHT})] * 2,
    10: [({0: RIGHT, 1: RIGHT}, {3: RIGHT})] * 2,
    11: [({0: RIGHT, 1: RIGHT}, {})] * 2,
    12: [({0: LEFT, 1: LEFT, 2: LEFT}, {})] * 2,
    13: [({0: RIGHT, 1: LEFT, 2: LEFT}, {})] * 2,
    14: [({0: RIGHT, 1: RIGHT, 2: RIGHT}, {})] * 2,
    15: [({1: BOTH, 2: BOTH}, {})] * 2,
}

SPLITS = {7: 3}

PLAN = {
    (0, 0): (
        [(0, 22), (4, 23), (10, 12), (14, 13), (18, 6), (23, 20), (27, 4), (35, 21), (42, 15), (49, 5), (54, 7)],
        [(2, 14), (6, 9), (13, 25), (17, 19), (24, 24), (29, 10), (33, 18), (39, 17), (43, 8), (49, 16), (56, 11)],
        [],
        [(31, 2), (44, 3), (48, 0), (56, 1)],
    ),
    (0, 1): (
        [(0, 14), (5, 9), (9, 25), (13, 19), (20, 24), (26, 10), (30, 18), (34, 17), (42, 8), (48, 16), (52, 11)],
        [(0, 29), (7, 26), (11, 28), (15, 22), (22, 13), (26, 23), (30, 12), (34, 27), (40, 20), (46, 21), (50, 15)],
        [],
        [(43, 4), (47, 6), (52, 5), (56, 7)],
    ),
    (1, 0): (
        [(0, 28), (4, 13), (8, 22), (12, 23), (18, 20), (25, 29), (29, 14), (33, 12), (42, 21), (50, 15)],
        [(1, 30), (5, 31), (10, 25), (14, 19), (18, 26), (24, 24), (28, 18), (39, 17), (44, 27), (51, 16)],
        [(17, 2), (28, 0), (35, 3), (43, 1)],
        [(39, 10), (45, 9), (49, 8), (53, 11)],
    ),
    (1, 1): (
        [(1, 17), (5, 2), (9, 25), (13, 24), (18, 26), (24, 0), (31, 3), (35, 1), (43, 27), (47, 16)],
        [(0, 31), (5, 19), (10, 28), (16, 22), (22, 30), (28, 18), (35, 29), (41, 23), (45, 20), (55, 21)],
        [(25, 4), (31, 6), (45, 5), (54, 7)],
        [(35, 13), (39, 14), (51, 12), (56, 15)],
    ),
    (2, 0): (
        [(0, 6), (4, 4), (8, 22), (12, 28), (21, 5), (25, 7), (37, 29), (43, 23), (47, 21), (51, 20)],
        [(10, 31), (14, 25), (26, 26), (33, 30), (37, 24), (53, 27)],
        [(5, 0), (10, 2), (15, 14), (23, 1), (27, 3), (38, 10), (42, 9), (46, 8), (53, 11)],
        [(47, 19), (51, 18), (55, 17), (59, 16)],
    ),
    (2, 1): (
        [(0, 26), (4, 24), (9, 25), (14, 9), (20, 10), (25, 8), (34, 27), (38, 19), (42, 11), (47, 18)],
        [(16, 31), (37, 28), (43, 29), (47, 30)],
        [(0, 0), (4, 2), (8, 1), (12, 3), (22, 6), (26, 4), (31, 13), (37, 12), (42, 5), (47, 7), (51, 15)],
        [(43, 22), (47, 23), (52, 20), (56, 21)],
    ),
    (3, 0): (
        [(0, 5), (4, 6), (9, 4), (13, 13), (17, 12), (24, 28), (29, 31), (35, 7), (40, 15), (47, 30), (53, 29)],
        [],
        [(3, 2), (7, 0), (12, 14), (16, 11), (22, 1), (27, 3), (34, 10), (40, 9), (46, 8), (50, 16), (54, 17)],
        [(40, 26), (46, 24), (50, 25), (56, 27)],
    ),
    (3, 1): (
        [(0, 2), (4, 0), (8, 14), (13, 11), (19, 1), (23, 3), (27, 10), (32, 9), (36, 8), (44, 16), (50, 17)],
        [],
        [(0, 19), (4, 5), (8, 18), (20, 6), (24, 4), (29, 13), (33, 12), (39, 20), (43, 7), (47, 15), (54, 21)],
        [(39, 31), (44, 28), (51, 30), (55, 29)],
    ),
}


def pieces(unit, per_tile):
    cut = SPLITS.get(unit // 2, 4) * per_tile // 8
    return (cut, per_tile - cut) if unit % 2 else (0, cut)


def device_steps(depth, panels):
    steps = {(z, x): {} for z in range(depth) for x in range(PAIR)}

    def plane(z, unit, leaves, onward, arriving):
        own = [(unit // 2 - panels * (PAIR * z + x)) % SITE_TILES <= LAST_OFFSET for x in range(PAIR)]
        held = [x for x in range(PAIR) if own[x] or arriving.get(x)]
        for x in held:
            if x not in leaves:
                steps[z, x][unit] = (own[x], tuple(arriving.get(x, ())), CROSS)
        crossed = (CROSS,) if any(x not in leaves for x in held) else ()
        for x in leaves:
            steps[z, x][unit] = (own[x], tuple(arriving.get(x, ())) + crossed, onward)

    for row, halves in ROUTES.items():
        home, column = row // (panels * PAIR), row // panels % PAIR
        for half, (rising, falling) in enumerate(halves):
            unit, merged = 2 * row + half, {}
            for onward, path, planes in ((UP, rising, range(home)), (DOWN, falling, range(depth - 1, home, -1))):
                arriving = {}
                for z in planes:
                    if z in path:
                        plane(z, unit, path[z], onward, arriving)
                        arriving = {x: (onward,) for x in path[z]}
                for x, kinds in arriving.items():
                    merged[x] = merged.get(x, ()) + kinds
            plane(home, unit, (column,), KEEP, merged)
    return steps


def stream_words(depth, panels, per_tile):
    steps = device_steps(depth, panels)

    def target(device, way):
        z, x = device
        return {CROSS: (z, 1 - x), UP: (z + 1, x), DOWN: (z - 1, x)}[way]

    bases, sent = {}, {}
    for device, streams in PLAN.items():
        for way in (CROSS, UP, DOWN):
            base = 0
            for _, unit in streams[way]:
                assert steps[device][unit][2] == way
                bases[target(device, way), unit, way] = base
                base += pieces(unit, per_tile)[1]
            sent[device, way] = base
    words = {}
    for device, streams in PLAN.items():
        planned = [unit for stream in streams for _, unit in stream]
        assert sorted(planned) == sorted(steps[device])
        origin, words[device] = panels * (PAIR * device[0] + device[1]), []
        for way, stream in enumerate(streams):
            line, free = [], 0
            for start, unit in stream:
                own, arriving, onward = steps[device][unit]
                begin, length = pieces(unit, per_tile)
                start = start * per_tile // 8
                assert onward == way and start >= free
                free = start + length
                base = 0 if way == KEEP else bases[target(device, way), unit, way]
                one = (unit // 2 - origin) % SITE_TILES + 16 * begin + 128 * base
                two = sum((1 + 2 * bases[device, unit, kind]) * 128**kind for kind in arriving)
                line.append((start, length, one, two))
            words[device].append(line)
        own, arriving, _ = steps[device][streams[CROSS][0][1]]
        assert own and not arriving
    return words, sent


def field_kernel(
    words, sent, own_reals, block_rows, eps_in, factor_in, median, spread, critical, field, mean_out,
    eps, factor, head, x_out, u_out, d_out, x_in, u_in, d_in, spare, totals, columns, folds, table,
    load_sem, x_send, u_send, d_send, x_recv, u_recv, d_recv, t_send, t_recv,
):
    panels, per_column, tile = factor.shape[0], factor.shape[1], factor.shape[2]
    depth = len(words) // PAIR
    count = PAIR * depth
    per_tile = tile // ROWS
    lines = panels * tile // LANES
    reals = lax.axis_size("real")
    site = lax.axis_index("site")
    me = lax.axis_index("real")
    z, x = site // PAIR, site % PAIR
    here = {device: site == device[0] * PAIR + device[1] for device in words}

    def pick(values):
        result = None
        for device, value in values.items():
            value = jnp.int32(value)
            result = value if result is None else jnp.where(here[device], value, result)
        return result

    begin = pick({device: own[CROSS][0][2] // 16 % 8 * ROWS for device, own in words.items()})
    first = [pltpu.make_async_copy(eps_in, eps, load_sem.at[0])]
    rest = []
    for panel in range(panels):
        first.append(pltpu.make_async_copy(
            factor_in.at[panel, :, pl.ds(pl.multiple_of(begin, ROWS), head.shape[2]), :],
            head.at[panel], load_sem.at[1 + panel],
        ))
        rest.append(pltpu.make_async_copy(
            factor_in.at[panel], factor.at[panel], load_sem.at[1 + panels + panel]
        ))
    for load in first + rest:
        load.start()

    barrier = pltpu.get_barrier_semaphore()
    pl.semaphore_signal(barrier, inc=1, device_id={"site": site + 1 - 2 * x}, device_id_type=MESH)
    for shift in range(1, reals):
        pl.semaphore_signal(barrier, inc=1, device_id={"real": (me + shift) % reals}, device_id_type=MESH)

    @pl.when(z > 0)
    def _():
        pl.semaphore_signal(barrier, inc=1, device_id={"site": site - PAIR}, device_id_type=MESH)

    @pl.when(z < depth - 1)
    def _():
        pl.semaphore_signal(barrier, inc=1, device_id={"site": site + PAIR}, device_id_type=MESH)

    plan, slots = [], 0
    for way in range(4):
        longest = max(len(own[way]) for own in words.values())
        pad = [(2**20, 0, 0, 0)] * longest
        plan.append([
            [pick({device: (own[way] + pad)[number][field] for device, own in words.items()}) for field in range(4)]
            for number in range(longest)
        ])
        slots = max([slots] + [own[way][-1][0] + own[way][-1][1] for own in words.values() if own[way]])

    for panel in range(panels):
        begins = [
            (block_rows[panel, block] - site * panels + panels * count) % (panels * count)
            for block in range(per_column)
        ]

        @pl.loop(0, table.shape[1])
        def _(slot):
            number, found = jnp.int32(0), jnp.int32(0)
            for block in range(per_column):
                hit = begins[block] == slot
                number = jnp.where(hit, block, number)
                found = jnp.where(hit, 1, found)
            table[panel, slot] = number
            table[panels + panel, slot] = found

    def bits(word, low, width):
        return lax.rem(lax.div(word, jnp.int32(2**low)), jnp.int32(2**width))

    def multiply(out, relative, piece, source):
        @pl.when(relative <= LAST_OFFSET)
        def _():
            row = pl.multiple_of(piece * ROWS, ROWS)
            result = None
            for panel in range(panels):
                block = source[panel, table[panel, relative], pl.ds(row, ROWS), :]
                product = jnp.dot(
                    block, eps[panel * tile:(panel + 1) * tile, :], preferred_element_type=jnp.float32
                ) * table[panels + panel, relative].astype(jnp.float32)
                result = product if result is None else result + product
            out[...] = result

        @pl.when(relative > LAST_OFFSET)
        def _():
            out[...] = jnp.zeros_like(out)

    ways = (
        (x_out, x_in, x_send, x_recv, site + 1 - 2 * x),
        (u_out, u_in, u_send, u_recv, (site + PAIR) % count),
        (d_out, d_in, d_send, d_recv, (site + count - PAIR) % count),
    )

    def copy(way, slot):
        leaving, landing, departure, arrival, there = ways[way]
        return pltpu.make_async_remote_copy(
            src_ref=leaving.at[slot],
            dst_ref=landing.at[slot],
            send_sem=departure.at[slot],
            recv_sem=arrival.at[slot],
            device_id={"site": there},
            device_id_type=MESH,
        )

    def keep(chunk):
        rounded = spare[...].astype(jnp.bfloat16)
        rows = pl.ds(pl.multiple_of(chunk * ROWS, ROWS), ROWS)
        field[rows, :] = rounded
        folded = None
        for piece in range(own_reals // LANES):
            residual = rounded[:, piece * LANES:(piece + 1) * LANES].astype(jnp.float32)
            log_peak = columns[0, rows, :] + columns[1, rows, :] * residual
            log_ratio = columns[2, rows, :] - log_peak
            margin = jnp.maximum(1.0 - jnp.exp(log_ratio), 0.0)
            displacement = coeff_disp * jnp.exp(power_margin * jnp.log(margin) - power_ratio * log_ratio)
            damage = jnp.log1p(displacement)
            folded = damage if folded is None else folded + damage
        folds[rows, :] = folded

        @pl.when((chunk + 1) % (LANES // ROWS) == 0)
        def _():
            line = chunk // (LANES // ROWS)
            group = folds[pl.ds(pl.multiple_of(line * LANES, LANES), LANES), :]
            totals[me, pl.ds(line, 1), :] = jnp.sum(group.T, axis=0, keepdims=True)

    def step(way, slot, least=0):
        turn, count, one, two = jnp.int32(0), jnp.int32(0), jnp.int32(0), jnp.int32(0)
        for start, length, first_word, second_word in plan[way]:
            later = slot >= start
            turn = jnp.where(later, slot - start, turn)
            count = jnp.where(later, length, count)
            one = jnp.where(later, first_word, one)
            two = jnp.where(later, second_word, two)

        @pl.when(jnp.logical_and(turn < count, slot >= least))
        def _():
            relative = bits(one, 0, 4)
            piece = bits(one, 4, 3) + turn
            place = bits(one, 7, 6) + turn
            out = spare if way == KEEP else ways[way][0].at[place]
            multiply(out, relative, piece, factor)
            for kind in range(3):
                @pl.when(bits(two, 7 * kind, 1) == 1)
                def _():
                    arrived = bits(two, 7 * kind + 1, 6) + turn
                    copy(kind, arrived).wait_recv()
                    out[...] = out[...] + ways[kind][1][arrived]

            if way == KEEP:
                keep(relative * per_tile + piece)
            else:
                copy(way, place).start()

    for load in first:
        load.wait()
    for turn in range(HEAD):
        multiply(x_out.at[turn], bits(plan[CROSS][0][2], 0, 4), turn, head)
    pl.semaphore_wait(barrier, reals + jnp.where(z > 0, 1, 0) + jnp.where(z < depth - 1, 1, 0))
    for turn in range(HEAD):
        copy(CROSS, turn).start()
    for load in rest:
        load.wait()

    @pl.loop(0, slots)
    def _(slot):
        step(CROSS, slot, plan[CROSS][0][0] + HEAD)

        @pl.when(slot < lines)
        def _():
            spot = pl.ds(pl.multiple_of(slot * LANES, LANES), LANES)
            for index, ref in enumerate((median, spread, critical)):
                value = ref[pl.ds(slot, 1), :]
                value = jnp.log(value) if index == 2 else value
                columns[index, spot, :] = jnp.broadcast_to(value, (LANES, LANES)).T

        for way in (UP, DOWN, KEEP):
            step(way, slot)

    def t_copy(shift):
        return pltpu.make_async_remote_copy(
            src_ref=totals.at[me],
            dst_ref=totals.at[me],
            send_sem=t_send.at[shift],
            recv_sem=t_recv.at[shift],
            device_id={"real": (me + shift) % reals},
            device_id_type=MESH,
        )

    for shift in range(1, reals):
        t_copy(shift).start()

    for way in (CROSS, UP, DOWN):
        @pl.loop(0, pick({device: sent[device, way] for device in words}))
        def _(slot):
            copy(way, slot).wait_send()

    for shift in range(1, reals):
        t_copy(shift).wait()
    total = totals[0]
    for source in range(1, reals):
        total = total + totals[source]
    mean_out[...] = total / (own_reals * reals)


def hand_out_kernel(field, mean, field_out, mean_out, out_sem):
    part = field.shape[0] // PARTS
    writes = [pltpu.make_async_copy(mean, mean_out, out_sem.at[PARTS])]
    for index in range(PARTS):
        rows = pl.ds(index * part, part)
        writes.append(pltpu.make_async_copy(field.at[rows, :], field_out.at[rows, :], out_sem.at[index]))
    for write in writes:
        write.start()
    for write in writes:
        write.wait()


def line_shards(epsilon, factor, block_rows, median_log, spread_log, critical_yield):
    panels, per_column, tile = factor.shape[:3]
    sites, own_reals = epsilon.shape
    count, reals = lax.axis_size("site"), lax.axis_size("real")
    lines = sites // LANES
    words, sent = stream_words(count // PAIR, panels, tile // ROWS)
    most = [max(sent[device, way] for device in words) for way in (CROSS, UP, DOWN)]
    piece = (ROWS, own_reals)
    vmem = pl.BlockSpec(memory_space=pltpu.VMEM)
    anywhere = pl.BlockSpec(memory_space=pl.ANY)
    field, mean = pl.pallas_call(
        functools.partial(field_kernel, words, sent, own_reals),
        out_shape=(
            pltpu.VMEM((sites, own_reals), jnp.bfloat16),
            pltpu.VMEM((lines, LANES), jnp.float32),
        ),
        in_specs=[pl.BlockSpec(memory_space=pltpu.SMEM), anywhere, anywhere, vmem, vmem, vmem],
        out_specs=(vmem, vmem),
        scratch_shapes=[
            pltpu.VMEM(epsilon.shape, epsilon.dtype),
            pltpu.VMEM(factor.shape, factor.dtype),
            pltpu.VMEM((panels, per_column, HEAD * ROWS, tile), factor.dtype),
            *[pltpu.VMEM((slots,) + piece, jnp.float32) for slots in most + most],
            pltpu.VMEM(piece, jnp.float32),
            pltpu.VMEM((reals, lines, LANES), jnp.float32),
            pltpu.VMEM((3, sites, LANES), jnp.float32),
            pltpu.VMEM((sites, LANES), jnp.float32),
            pltpu.SMEM((2 * panels, SITE_TILES), jnp.int32),
            pltpu.SemaphoreType.DMA((1 + 2 * panels,)),
            *[pltpu.SemaphoreType.DMA((slots,)) for slots in most + most],
            pltpu.SemaphoreType.DMA((reals,)),
            pltpu.SemaphoreType.DMA((reals,)),
        ],
        compiler_params=pltpu.CompilerParams(
            collective_id=0, has_side_effects=True, vmem_limit_bytes=60 * 1024 * 1024
        ),
    )(
        block_rows,
        epsilon,
        factor,
        median_log.reshape(lines, LANES),
        spread_log.reshape(lines, LANES),
        critical_yield.reshape(lines, LANES),
    )
    field, mean = pl.pallas_call(
        hand_out_kernel,
        out_shape=(
            jax.ShapeDtypeStruct(field.shape, field.dtype),
            jax.ShapeDtypeStruct(mean.shape, mean.dtype),
        ),
        in_specs=[vmem, vmem],
        out_specs=(anywhere, anywhere),
        scratch_shapes=[pltpu.SemaphoreType.DMA((PARTS + 1,))],
    )(pltpu.with_memory_space_constraint(field, pltpu.VMEM), pltpu.with_memory_space_constraint(mean, pltpu.VMEM))
    return field, mean.reshape(sites)


def solution(mesh):
    body = line_shards if mesh.shape["site"] == BAND // 2 + PAIR else shards
    return jax.shard_map(
        body,
        mesh=mesh,
        in_specs=(
            P("site", "real"),
            P(None, "site", None, None),
            P(None, "site"),
            P("site"),
            P("site"),
            P("site"),
        ),
        out_specs=(P("site", "real"), P("site")),
        check_vma=False,
    )
```

```python
import functools
import jax
import jax.numpy as jnp
from jax import lax
from jax.experimental import pallas as pl
from jax.experimental.pallas import tpu as pltpu
from jax.sharding import PartitionSpec as P

BAND = 12
PAIR = 2
LANES = 128
ROWS = 64
PARTS = 4
HEAD = 2
LEAD = 3
SITE_TILES = 16
LAST_OFFSET = 12
CROSS, UP, DOWN, KEEP = range(4)
MESH = pl.DeviceIdType.MESH

coeff_disp = 10.0**0.215
power_margin = 2.341
power_ratio = 1.438


def passed_along(value, axis, steps):
    count = lax.axis_size(axis)
    pairs = [(source, (source + steps) % count) for source in range(count)]
    return lax.ppermute(value, axis, pairs)


def shards(epsilon, factor, block_rows, median_log, spread_log, critical_yield):
    panels = factor.shape[0]
    per_column = factor.shape[1]
    tile_size = factor.shape[-1]
    own_reals = epsilon.shape[1]
    reach = BAND // 2
    own_index = lax.axis_index("site")
    total_tiles = panels * lax.axis_size("site")
    draws = epsilon.reshape(panels, tile_size, own_reals)

    def pending(panel):
        flat = factor[panel].reshape(per_column * tile_size, tile_size)
        products = jnp.dot(flat, draws[panel], preferred_element_type=jnp.float32)
        products = products.reshape(per_column, tile_size, own_reals)
        relative = (block_rows[panel] - own_index * panels) % total_tiles
        slots = jnp.zeros(((reach + 1) * panels, tile_size, own_reals), jnp.float32)
        sums = slots.at[relative].set(products, unique_indices=True)
        return sums.reshape(reach + 1, panels, tile_size, own_reals)

    combined = pending(0)
    panel = 1
    combined = combined + pending(panel)
    arrived = combined[0]
    for offset in range(1, reach + 1):
        arrived = arrived + passed_along(combined[offset], "site", offset)
    residual_field = arrived.astype(jnp.bfloat16).reshape(panels * tile_size, own_reals)
    log_peak = median_log[:, None] + spread_log[:, None] * residual_field.astype(jnp.float32)
    log_ratio = jnp.log(critical_yield)[:, None] - log_peak
    ratio = jnp.exp(log_ratio)
    margin = jnp.maximum(1.0 - ratio, 0.0)
    displacement = coeff_disp * jnp.power(margin, power_margin) * jnp.exp(-power_ratio * log_ratio)
    local_total = jnp.sum(jnp.log1p(displacement), axis=1)
    total = lax.psum(local_total, "real")
    mean_damage = total / (own_reals * lax.axis_size("real"))
    return (residual_field, mean_damage)

LEFT, RIGHT, BOTH = (0,), (1,), (0, 1)
ROUTES = {
    0: [({}, {3: LEFT, 2: BOTH, 1: LEFT})] * 2,
    1: [({}, {3: LEFT, 2: BOTH, 1: LEFT})] * 2,
    2: [({}, {3: RIGHT, 2: RIGHT, 1: RIGHT})] * 2,
    3: [({}, {3: RIGHT, 2: RIGHT, 1: RIGHT})] * 2,
    4: [({0: LEFT}, {3: LEFT, 2: LEFT})] * 2,
    5: [({0: LEFT}, {3: LEFT, 2: LEFT})] * 2,
    6: [({0: RIGHT}, {3: RIGHT, 2: RIGHT})] * 2,
    7: [({0: LEFT}, {3: LEFT, 2: LEFT}), ({0: RIGHT}, {3: RIGHT, 2: RIGHT})],
    8: [({0: LEFT, 1: LEFT}, {3: LEFT})] * 2,
    9: [({0: LEFT, 1: BOTH}, {3: RIGHT})] * 2,
    10: [({0: RIGHT, 1: RIGHT}, {3: RIGHT})] * 2,
    11: [({0: RIGHT, 1: RIGHT}, {})] * 2,
    12: [({0: LEFT, 1: LEFT, 2: LEFT}, {})] * 2,
    13: [({0: RIGHT, 1: LEFT, 2: LEFT}, {})] * 2,
    14: [({0: RIGHT, 1: RIGHT, 2: RIGHT}, {})] * 2,
    15: [({1: BOTH, 2: BOTH}, {})] * 2,
}

SPLITS = {7: 3}

PLAN = {
    (0, 0): (
        [(0, 20), (4, 22), (10, 21), (15, 15), (20, 23), (27, 5), (36, 12), (42, 13), (46, 7), (50, 4), (54, 6)],
        [(4, 25), (8, 10), (15, 18), (20, 19), (27, 24), (35, 14), (38, 11), (43, 8), (47, 17), (51, 16), (55, 9)],
        [],
        [(33, 0), (42, 2), (51, 1), (55, 3)],
    ),
    (0, 1): (
        [(0, 25), (4, 10), (8, 18), (12, 19), (20, 24), (28, 14), (31, 11), (35, 8), (39, 17), (43, 16), (47, 9)],
        [(2, 27), (6, 26), (15, 29), (19, 28), (26, 22), (30, 23), (34, 21), (38, 12), (42, 20), (46, 13), (51, 15)],
        [],
        [(39, 5), (46, 7), (51, 4), (56, 6)],
    ),
    (1, 0): (
        [(3, 28), (7, 22), (11, 20), (17, 23), (23, 12), (30, 29), (35, 21), (45, 14), (48, 13), (52, 15)],
        [(0, 30), (6, 31), (12, 26), (17, 27), (21, 19), (29, 18), (36, 24), (42, 25), (49, 17), (54, 16)],
        [(18, 0), (35, 2), (44, 1), (54, 3)],
        [(37, 11), (44, 8), (48, 10), (56, 9)],
    ),
    (1, 1): (
        [(2, 24), (8, 27), (12, 26), (16, 0), (20, 25), (24, 2), (28, 16), (32, 1), (39, 17), (48, 3)],
        [(1, 30), (5, 19), (13, 18), (18, 31), (25, 28), (32, 23), (36, 29), (40, 22), (46, 20), (53, 21)],
        [(30, 5), (35, 7), (42, 6), (50, 4)],
        [(42, 12), (47, 14), (50, 13), (54, 15)],
    ),
    (2, 0): (
        [(0, 7), (4, 28), (9, 6), (13, 22), (18, 5), (24, 23), (29, 29), (36, 4), (46, 20), (52, 21)],
        [(10, 31), (14, 30), (22, 27), (37, 26), (48, 25), (54, 24)],
        [(8, 0), (12, 11), (18, 14), (21, 1), (27, 2), (37, 8), (43, 10), (50, 3), (54, 9)],
        [(47, 19), (51, 18), (55, 17), (59, 16)],
    ),
    (2, 1): (
        [(0, 27), (4, 11), (8, 25), (12, 8), (19, 10), (28, 24), (34, 26), (40, 19), (49, 18), (53, 9)],
        [(5, 30), (32, 28), (36, 31), (44, 29)],
        [(0, 1), (4, 2), (8, 0), (13, 6), (20, 3), (29, 5), (33, 7), (38, 12), (42, 13), (48, 4), (52, 15)],
        [(40, 23), (48, 22), (52, 20), (56, 21)],
    ),
    (3, 0): (
        [(0, 5), (4, 6), (8, 12), (14, 31), (21, 7), (27, 13), (31, 15), (38, 4), (42, 28), (46, 29), (52, 30)],
        [],
        [(2, 0), (6, 11), (13, 1), (21, 14), (26, 2), (32, 10), (37, 8), (41, 9), (45, 3), (49, 17), (53, 16)],
        [(43, 26), (47, 27), (51, 25), (55, 24)],
    ),
    (3, 1): (
        [(0, 0), (4, 11), (10, 1), (14, 14), (17, 2), (21, 10), (27, 8), (31, 9), (38, 3), (44, 17), (48, 16)],
        [],
        [(0, 18), (4, 19), (8, 6), (12, 20), (22, 5), (26, 7), (30, 12), (34, 13), (39, 4), (44, 15), (54, 21)],
        [(37, 31), (44, 28), (52, 29), (56, 30)],
    ),
}


def pieces(unit, per_tile):
    cut = SPLITS.get(unit // 2, 4) * per_tile // 8
    return (cut, per_tile - cut) if unit % 2 else (0, cut)


def device_steps(depth, panels):
    steps = {(z, x): {} for z in range(depth) for x in range(PAIR)}

    def plane(z, unit, leaves, onward, arriving):
        own = [(unit // 2 - panels * (PAIR * z + x)) % SITE_TILES <= LAST_OFFSET for x in range(PAIR)]
        held = [x for x in range(PAIR) if own[x] or arriving.get(x)]
        for x in held:
            if x not in leaves:
                steps[z, x][unit] = (own[x], tuple(arriving.get(x, ())), CROSS)
        crossed = (CROSS,) if any(x not in leaves for x in held) else ()
        for x in leaves:
            steps[z, x][unit] = (own[x], tuple(arriving.get(x, ())) + crossed, onward)

    for row, halves in ROUTES.items():
        home, column = row // (panels * PAIR), row // panels % PAIR
        for half, (rising, falling) in enumerate(halves):
            unit, merged = 2 * row + half, {}
            for onward, path, planes in ((UP, rising, range(home)), (DOWN, falling, range(depth - 1, home, -1))):
                arriving = {}
                for z in planes:
                    if z in path:
                        plane(z, unit, path[z], onward, arriving)
                        arriving = {x: (onward,) for x in path[z]}
                for x, kinds in arriving.items():
                    merged[x] = merged.get(x, ()) + kinds
            plane(home, unit, (column,), KEEP, merged)
    return steps


def stream_words(depth, panels, per_tile):
    steps = device_steps(depth, panels)

    def target(device, way):
        z, x = device
        return {CROSS: (z, 1 - x), UP: (z + 1, x), DOWN: (z - 1, x)}[way]

    bases, sent = {}, {}
    for device, streams in PLAN.items():
        for way in (CROSS, UP, DOWN):
            base = 0
            for _, unit in streams[way]:
                assert steps[device][unit][2] == way
                bases[target(device, way), unit, way] = base
                base += pieces(unit, per_tile)[1]
            sent[device, way] = base
    words, leads = {}, {}
    for device, streams in PLAN.items():
        planned = [unit for stream in streams for _, unit in stream]
        assert sorted(planned) == sorted(steps[device])
        origin, words[device] = panels * (PAIR * device[0] + device[1]), []
        for way, stream in enumerate(streams):
            line, free = [], 0
            for start, unit in stream:
                own, arriving, onward = steps[device][unit]
                begin, length = pieces(unit, per_tile)
                start = start * per_tile // 8
                assert onward == way and start >= free
                free = start + length
                base = 0 if way == KEEP else bases[target(device, way), unit, way]
                one = (unit // 2 - origin) % SITE_TILES + 16 * begin + 128 * base
                two = sum((1 + 2 * bases[device, unit, kind]) * 128**kind for kind in arriving)
                line.append((start, length, one, two))
            words[device].append(line)
        for way in (CROSS, UP, DOWN):
            start, unit = (streams[way] or [(2**20, 0)])[0]
            own, arriving, _ = steps[device].get(unit, (False, (), way))
            leads[device, way] = own and not arriving and start <= LEAD
            assert not leads[device, way] or pieces(unit, per_tile)[0] == pieces(streams[CROSS][0][1], per_tile)[0]
    return words, sent, leads


def field_kernel(
    words, sent, leads, own_reals, rows_in, eps_in, factor_in, median_in, spread_in, critical_in, field, mean_out,
    block_rows, sites_in, eps, factor, head, x_out, u_out, d_out, x_in, u_in, d_in, spare, totals, columns, folds, table,
    load_sem, site_sem, x_send, u_send, d_send, x_recv, u_recv, d_recv, t_send, t_recv,
):
    panels, per_column, tile = factor.shape[0], factor.shape[1], factor.shape[2]
    depth = len(words) // PAIR
    count = PAIR * depth
    per_tile = tile // ROWS
    lines = panels * tile // LANES
    reals = lax.axis_size("real")
    site = lax.axis_index("site")
    me = lax.axis_index("real")
    z, x = site // PAIR, site % PAIR
    here = {device: site == device[0] * PAIR + device[1] for device in words}

    def pick(values):
        result = None
        for device, value in values.items():
            value = jnp.int32(value)
            result = value if result is None else jnp.where(here[device], value, result)
        return result

    barrier = pltpu.get_barrier_semaphore()
    pl.semaphore_signal(barrier, inc=1, device_id={"site": site + 1 - 2 * x}, device_id_type=MESH)
    for shift in range(1, reals):
        pl.semaphore_signal(barrier, inc=1, device_id={"real": (me + shift) % reals}, device_id_type=MESH)

    @pl.when(z > 0)
    def _():
        pl.semaphore_signal(barrier, inc=1, device_id={"site": site - PAIR}, device_id_type=MESH)

    @pl.when(z < depth - 1)
    def _():
        pl.semaphore_signal(barrier, inc=1, device_id={"site": site + PAIR}, device_id_type=MESH)

    begin = pick({device: own[CROSS][0][2] // 16 % 8 * ROWS for device, own in words.items()})
    first = [pltpu.make_async_copy(eps_in, eps, load_sem.at[0])]
    rest = []
    for panel in range(panels):
        first.append(pltpu.make_async_copy(
            factor_in.at[panel, :, pl.ds(pl.multiple_of(begin, ROWS), head.shape[2]), :],
            head.at[panel], load_sem.at[1 + panel],
        ))
        rest.append(pltpu.make_async_copy(
            factor_in.at[panel], factor.at[panel], load_sem.at[1 + panels + panel]
        ))
    known = [pltpu.make_async_copy(rows_in, block_rows, site_sem.at[0])]
    for index, ref in enumerate((median_in, spread_in, critical_in)):
        known.append(pltpu.make_async_copy(ref, sites_in.at[index], site_sem.at[1 + index]))
    for load in known + first + rest:
        load.start()

    plan, slots = [], 0
    for way in range(4):
        longest = max(len(own[way]) for own in words.values())
        pad = [(2**20, 0, 0, 0)] * longest
        plan.append([
            [pick({device: (own[way] + pad)[number][field] for device, own in words.items()}) for field in range(4)]
            for number in range(longest)
        ])
        slots = max([slots] + [own[way][-1][0] + own[way][-1][1] for own in words.values() if own[way]])

    for load in known:
        load.wait()
    for panel in range(panels):
        begins = [
            (block_rows[panel, block] - site * panels + panels * count) % (panels * count)
            for block in range(per_column)
        ]

        @pl.loop(0, table.shape[1])
        def _(slot):
            number, found = jnp.int32(0), jnp.int32(0)
            for block in range(per_column):
                hit = begins[block] == slot
                number = jnp.where(hit, block, number)
                found = jnp.where(hit, 1, found)
            table[panel, slot] = number
            table[panels + panel, slot] = found

    def bits(word, low, width):
        return lax.rem(lax.div(word, jnp.int32(2**low)), jnp.int32(2**width))

    def multiply(out, relative, piece, source):
        @pl.when(relative <= LAST_OFFSET)
        def _():
            row = pl.multiple_of(piece * ROWS, ROWS)
            result = None
            for panel in range(panels):
                block = source[panel, table[panel, relative], pl.ds(row, ROWS), :]
                product = jnp.dot(
                    block, eps[panel * tile:(panel + 1) * tile, :], preferred_element_type=jnp.float32
                ) * table[panels + panel, relative].astype(jnp.float32)
                result = product if result is None else result + product
            out[...] = result

        @pl.when(relative > LAST_OFFSET)
        def _():
            out[...] = jnp.zeros_like(out)

    ways = (
        (x_out, x_in, x_send, x_recv, site + 1 - 2 * x),
        (u_out, u_in, u_send, u_recv, (site + PAIR) % count),
        (d_out, d_in, d_send, d_recv, (site + count - PAIR) % count),
    )

    def copy(way, slot):
        leaving, landing, departure, arrival, there = ways[way]
        return pltpu.make_async_remote_copy(
            src_ref=leaving.at[slot],
            dst_ref=landing.at[slot],
            send_sem=departure.at[slot],
            recv_sem=arrival.at[slot],
            device_id={"site": there},
            device_id_type=MESH,
        )

    def keep(chunk):
        rounded = spare[...].astype(jnp.bfloat16)
        rows = pl.ds(pl.multiple_of(chunk * ROWS, ROWS), ROWS)
        field[rows, :] = rounded
        folded = None
        for piece in range(own_reals // LANES):
            residual = rounded[:, piece * LANES:(piece + 1) * LANES].astype(jnp.float32)
            log_peak = columns[0, rows, :] + columns[1, rows, :] * residual
            log_ratio = columns[2, rows, :] - log_peak
            margin = jnp.maximum(1.0 - jnp.exp(log_ratio), 0.0)
            displacement = coeff_disp * jnp.exp(power_margin * jnp.log(margin) - power_ratio * log_ratio)
            damage = jnp.log1p(displacement)
            folded = damage if folded is None else folded + damage
        folds[rows, :] = folded

        @pl.when((chunk + 1) % (LANES // ROWS) == 0)
        def _():
            line = chunk // (LANES // ROWS)
            group = folds[pl.ds(pl.multiple_of(line * LANES, LANES), LANES), :]
            totals[me, pl.ds(line, 1), :] = jnp.sum(group.T, axis=0, keepdims=True)

    def step(way, slot, least=0):
        turn, count, one, two = jnp.int32(0), jnp.int32(0), jnp.int32(0), jnp.int32(0)
        for start, length, first_word, second_word in plan[way]:
            later = slot >= start
            turn = jnp.where(later, slot - start, turn)
            count = jnp.where(later, length, count)
            one = jnp.where(later, first_word, one)
            two = jnp.where(later, second_word, two)

        @pl.when(jnp.logical_and(turn < count, slot >= least))
        def _():
            relative = bits(one, 0, 4)
            piece = bits(one, 4, 3) + turn
            place = bits(one, 7, 6) + turn
            out = spare if way == KEEP else ways[way][0].at[place]
            multiply(out, relative, piece, factor)
            for kind in range(3):
                @pl.when(bits(two, 7 * kind, 1) == 1)
                def _():
                    arrived = bits(two, 7 * kind + 1, 6) + turn
                    copy(kind, arrived).wait_recv()
                    out[...] = out[...] + ways[kind][1][arrived]

            if way == KEEP:
                keep(relative * per_tile + piece)
            else:
                copy(way, place).start()

    for load in first:
        load.wait()
    ahead = [pick({device: leads[device, way] for device in words}) for way in (CROSS, UP, DOWN)]
    for turn in range(HEAD):
        for way in (CROSS, UP, DOWN):
            @pl.when(ahead[way] == 1)
            def _():
                multiply(ways[way][0].at[turn], bits(plan[way][0][2], 0, 4), turn, head)

        if turn == 0:
            pl.semaphore_wait(barrier, reals + jnp.where(z > 0, 1, 0) + jnp.where(z < depth - 1, 1, 0))

        for way in (CROSS, UP, DOWN):
            @pl.when(ahead[way] == 1)
            def _():
                copy(way, turn).start()

    for load in rest:
        load.wait()

    @pl.loop(0, slots)
    def _(slot):
        step(CROSS, slot, plan[CROSS][0][0] + HEAD * ahead[CROSS])

        @pl.when(slot < lines)
        def _():
            spot = pl.ds(pl.multiple_of(slot * LANES, LANES), LANES)
            for index in range(3):
                value = sites_in[index, pl.ds(slot, 1), :]
                value = jnp.log(value) if index == 2 else value
                columns[index, spot, :] = jnp.broadcast_to(value, (LANES, LANES)).T

        for way in (UP, DOWN):
            step(way, slot, plan[way][0][0] + HEAD * ahead[way])
        step(KEEP, slot)

    def t_copy(shift):
        return pltpu.make_async_remote_copy(
            src_ref=totals.at[me],
            dst_ref=totals.at[me],
            send_sem=t_send.at[shift],
            recv_sem=t_recv.at[shift],
            device_id={"real": (me + shift) % reals},
            device_id_type=MESH,
        )

    for shift in range(1, reals):
        t_copy(shift).start()

    for way in (CROSS, UP, DOWN):
        @pl.loop(0, pick({device: sent[device, way] for device in words}))
        def _(slot):
            copy(way, slot).wait_send()

    for shift in range(1, reals):
        t_copy(shift).wait()
    total = totals[0]
    for source in range(1, reals):
        total = total + totals[source]
    mean_out[...] = total / (own_reals * reals)


def hand_out_kernel(field, mean, field_out, mean_out, out_sem):
    part = field.shape[0] // PARTS
    writes = [pltpu.make_async_copy(mean, mean_out, out_sem.at[PARTS])]
    for index in range(PARTS):
        rows = pl.ds(index * part, part)
        writes.append(pltpu.make_async_copy(field.at[rows, :], field_out.at[rows, :], out_sem.at[index]))
    for write in writes:
        write.start()
    for write in writes:
        write.wait()


def line_shards(epsilon, factor, block_rows, median_log, spread_log, critical_yield):
    panels, per_column, tile = factor.shape[:3]
    sites, own_reals = epsilon.shape
    count, reals = lax.axis_size("site"), lax.axis_size("real")
    lines = sites // LANES
    words, sent, leads = stream_words(count // PAIR, panels, tile // ROWS)
    most = [max(sent[device, way] for device in words) for way in (CROSS, UP, DOWN)]
    piece = (ROWS, own_reals)
    vmem = pl.BlockSpec(memory_space=pltpu.VMEM)
    anywhere = pl.BlockSpec(memory_space=pl.ANY)
    field, mean = pl.pallas_call(
        functools.partial(field_kernel, words, sent, leads, own_reals),
        out_shape=(
            pltpu.VMEM((sites, own_reals), jnp.bfloat16),
            pltpu.VMEM((lines, LANES), jnp.float32),
        ),
        in_specs=[anywhere] * 6,
        out_specs=(vmem, vmem),
        scratch_shapes=[
            pltpu.SMEM(block_rows.shape, block_rows.dtype),
            pltpu.VMEM((3, lines, LANES), jnp.float32),
            pltpu.VMEM(epsilon.shape, epsilon.dtype),
            pltpu.VMEM(factor.shape, factor.dtype),
            pltpu.VMEM((panels, per_column, HEAD * ROWS, tile), factor.dtype),
            *[pltpu.VMEM((slots,) + piece, jnp.float32) for slots in most + most],
            pltpu.VMEM(piece, jnp.float32),
            pltpu.VMEM((reals, lines, LANES), jnp.float32),
            pltpu.VMEM((3, sites, LANES), jnp.float32),
            pltpu.VMEM((sites, LANES), jnp.float32),
            pltpu.SMEM((2 * panels, SITE_TILES), jnp.int32),
            pltpu.SemaphoreType.DMA((1 + 2 * panels,)),
            pltpu.SemaphoreType.DMA((4,)),
            *[pltpu.SemaphoreType.DMA((slots,)) for slots in most + most],
            pltpu.SemaphoreType.DMA((reals,)),
            pltpu.SemaphoreType.DMA((reals,)),
        ],
        compiler_params=pltpu.CompilerParams(
            collective_id=0, has_side_effects=True, vmem_limit_bytes=60 * 1024 * 1024
        ),
    )(
        block_rows,
        epsilon,
        factor,
        median_log.reshape(lines, LANES),
        spread_log.reshape(lines, LANES),
        critical_yield.reshape(lines, LANES),
    )
    field, mean = pl.pallas_call(
        hand_out_kernel,
        out_shape=(
            jax.ShapeDtypeStruct(field.shape, field.dtype),
            jax.ShapeDtypeStruct(mean.shape, mean.dtype),
        ),
        in_specs=[vmem, vmem],
        out_specs=(anywhere, anywhere),
        scratch_shapes=[pltpu.SemaphoreType.DMA((PARTS + 1,))],
    )(pltpu.with_memory_space_constraint(field, pltpu.VMEM), pltpu.with_memory_space_constraint(mean, pltpu.VMEM))
    return field, mean.reshape(sites)


def solution(mesh):
    body = line_shards if mesh.shape["site"] == BAND // 2 + PAIR else shards
    return jax.shard_map(
        body,
        mesh=mesh,
        in_specs=(
            P("site", "real"),
            P(None, "site", None, None),
            P(None, "site"),
            P("site"),
            P("site"),
            P("site"),
        ),
        out_specs=(P("site", "real"), P("site")),
        check_vma=False,
    )
```

```python
import functools
import jax
import jax.numpy as jnp
from jax import lax
from jax.experimental import pallas as pl
from jax.experimental.pallas import tpu as pltpu
from jax.sharding import PartitionSpec as P

BAND = 12
PAIR = 2
LANES = 128
ROWS = 64
PARTS = 4
HEAD = 2
LEAD = 3
SITE_TILES = 16
LAST_OFFSET = 12
CROSS, UP, DOWN, KEEP = range(4)
MESH = pl.DeviceIdType.MESH

coeff_disp = 10.0**0.215
power_margin = 2.341
power_ratio = 1.438


def passed_along(value, axis, steps):
    count = lax.axis_size(axis)
    pairs = [(source, (source + steps) % count) for source in range(count)]
    return lax.ppermute(value, axis, pairs)


def shards(epsilon, factor, block_rows, median_log, spread_log, critical_yield):
    panels = factor.shape[0]
    per_column = factor.shape[1]
    tile_size = factor.shape[-1]
    own_reals = epsilon.shape[1]
    reach = BAND // 2
    own_index = lax.axis_index("site")
    total_tiles = panels * lax.axis_size("site")
    draws = epsilon.reshape(panels, tile_size, own_reals)

    def pending(panel):
        flat = factor[panel].reshape(per_column * tile_size, tile_size)
        products = jnp.dot(flat, draws[panel], preferred_element_type=jnp.float32)
        products = products.reshape(per_column, tile_size, own_reals)
        relative = (block_rows[panel] - own_index * panels) % total_tiles
        slots = jnp.zeros(((reach + 1) * panels, tile_size, own_reals), jnp.float32)
        sums = slots.at[relative].set(products, unique_indices=True)
        return sums.reshape(reach + 1, panels, tile_size, own_reals)

    combined = pending(0)
    panel = 1
    combined = combined + pending(panel)
    arrived = combined[0]
    for offset in range(1, reach + 1):
        arrived = arrived + passed_along(combined[offset], "site", offset)
    residual_field = arrived.astype(jnp.bfloat16).reshape(panels * tile_size, own_reals)
    log_peak = median_log[:, None] + spread_log[:, None] * residual_field.astype(jnp.float32)
    log_ratio = jnp.log(critical_yield)[:, None] - log_peak
    ratio = jnp.exp(log_ratio)
    margin = jnp.maximum(1.0 - ratio, 0.0)
    displacement = coeff_disp * jnp.power(margin, power_margin) * jnp.exp(-power_ratio * log_ratio)
    local_total = jnp.sum(jnp.log1p(displacement), axis=1)
    total = lax.psum(local_total, "real")
    mean_damage = total / (own_reals * lax.axis_size("real"))
    return (residual_field, mean_damage)

LEFT, RIGHT, BOTH = (0,), (1,), (0, 1)
ROUTES = {
    0: [({}, {3: LEFT, 2: BOTH, 1: LEFT})] * 2,
    1: [({}, {3: LEFT, 2: BOTH, 1: LEFT})] * 2,
    2: [({}, {3: RIGHT, 2: RIGHT, 1: RIGHT})] * 2,
    3: [({}, {3: RIGHT, 2: RIGHT, 1: RIGHT})] * 2,
    4: [({0: LEFT}, {3: LEFT, 2: LEFT})] * 2,
    5: [({0: LEFT}, {3: LEFT, 2: LEFT})] * 2,
    6: [({0: RIGHT}, {3: RIGHT, 2: RIGHT})] * 2,
    7: [({0: LEFT}, {3: LEFT, 2: LEFT}), ({0: RIGHT}, {3: RIGHT, 2: RIGHT})],
    8: [({0: LEFT, 1: LEFT}, {3: LEFT})] * 2,
    9: [({0: LEFT, 1: BOTH}, {3: RIGHT})] * 2,
    10: [({0: RIGHT, 1: RIGHT}, {3: RIGHT})] * 2,
    11: [({0: RIGHT, 1: RIGHT}, {})] * 2,
    12: [({0: LEFT, 1: LEFT, 2: LEFT}, {})] * 2,
    13: [({0: RIGHT, 1: LEFT, 2: LEFT}, {})] * 2,
    14: [({0: RIGHT, 1: RIGHT, 2: RIGHT}, {})] * 2,
    15: [({1: BOTH, 2: BOTH}, {})] * 2,
}

SPLITS = {7: 3}

PLAN = {
    (0, 0): (
        [(0, 20), (4, 22), (10, 21), (15, 15), (20, 23), (27, 5), (36, 12), (42, 13), (46, 7), (50, 4), (54, 6)],
        [(4, 25), (8, 10), (15, 18), (20, 19), (27, 24), (35, 14), (38, 11), (43, 8), (47, 17), (51, 16), (55, 9)],
        [],
        [(33, 0), (42, 2), (51, 1), (55, 3)],
    ),
    (0, 1): (
        [(0, 25), (4, 10), (8, 18), (12, 19), (20, 24), (28, 14), (31, 11), (35, 8), (39, 17), (43, 16), (47, 9)],
        [(2, 27), (6, 26), (15, 29), (19, 28), (26, 22), (30, 23), (34, 21), (38, 12), (42, 20), (46, 13), (51, 15)],
        [],
        [(39, 5), (46, 7), (51, 4), (56, 6)],
    ),
    (1, 0): (
        [(3, 28), (7, 22), (11, 20), (17, 23), (23, 12), (30, 29), (35, 21), (45, 14), (48, 13), (52, 15)],
        [(0, 30), (6, 31), (12, 26), (17, 27), (21, 19), (29, 18), (36, 24), (42, 25), (49, 17), (54, 16)],
        [(18, 0), (35, 2), (44, 1), (54, 3)],
        [(37, 11), (44, 8), (48, 10), (56, 9)],
    ),
    (1, 1): (
        [(2, 24), (8, 27), (12, 26), (16, 0), (20, 25), (24, 2), (28, 16), (32, 1), (39, 17), (48, 3)],
        [(1, 30), (5, 19), (13, 18), (18, 31), (25, 28), (32, 23), (36, 29), (40, 22), (46, 20), (53, 21)],
        [(30, 5), (35, 7), (42, 6), (50, 4)],
        [(42, 12), (47, 14), (50, 13), (54, 15)],
    ),
    (2, 0): (
        [(0, 7), (4, 28), (9, 6), (13, 22), (18, 5), (24, 23), (29, 29), (36, 4), (46, 20), (52, 21)],
        [(10, 31), (14, 30), (22, 27), (37, 26), (48, 25), (54, 24)],
        [(8, 0), (12, 11), (18, 14), (21, 1), (27, 2), (37, 8), (43, 10), (50, 3), (54, 9)],
        [(47, 19), (51, 18), (55, 17), (59, 16)],
    ),
    (2, 1): (
        [(0, 27), (4, 11), (8, 25), (12, 8), (19, 10), (28, 24), (34, 26), (40, 19), (49, 18), (53, 9)],
        [(5, 30), (32, 28), (36, 31), (44, 29)],
        [(0, 1), (4, 2), (8, 0), (13, 6), (20, 3), (29, 5), (33, 7), (38, 12), (42, 13), (48, 4), (52, 15)],
        [(40, 23), (48, 22), (52, 20), (56, 21)],
    ),
    (3, 0): (
        [(0, 5), (4, 6), (8, 12), (14, 31), (21, 7), (27, 13), (31, 15), (38, 4), (42, 28), (46, 29), (52, 30)],
        [],
        [(2, 0), (6, 11), (13, 1), (21, 14), (26, 2), (32, 10), (37, 8), (41, 9), (45, 3), (49, 17), (53, 16)],
        [(43, 26), (47, 27), (51, 25), (55, 24)],
    ),
    (3, 1): (
        [(0, 0), (4, 11), (10, 1), (14, 14), (17, 2), (21, 10), (27, 8), (31, 9), (38, 3), (44, 17), (48, 16)],
        [],
        [(0, 18), (4, 19), (8, 6), (12, 20), (22, 5), (26, 7), (30, 12), (34, 13), (39, 4), (44, 15), (54, 21)],
        [(37, 31), (44, 28), (52, 29), (56, 30)],
    ),
}


def pieces(unit, per_tile):
    cut = SPLITS.get(unit // 2, 4) * per_tile // 8
    return (cut, per_tile - cut) if unit % 2 else (0, cut)


def device_steps(depth, panels):
    steps = {(z, x): {} for z in range(depth) for x in range(PAIR)}

    def plane(z, unit, leaves, onward, arriving):
        own = [(unit // 2 - panels * (PAIR * z + x)) % SITE_TILES <= LAST_OFFSET for x in range(PAIR)]
        held = [x for x in range(PAIR) if own[x] or arriving.get(x)]
        for x in held:
            if x not in leaves:
                steps[z, x][unit] = (own[x], tuple(arriving.get(x, ())), CROSS)
        crossed = (CROSS,) if any(x not in leaves for x in held) else ()
        for x in leaves:
            steps[z, x][unit] = (own[x], tuple(arriving.get(x, ())) + crossed, onward)

    for row, halves in ROUTES.items():
        home, column = row // (panels * PAIR), row // panels % PAIR
        for half, (rising, falling) in enumerate(halves):
            unit, merged = 2 * row + half, {}
            for onward, path, planes in ((UP, rising, range(home)), (DOWN, falling, range(depth - 1, home, -1))):
                arriving = {}
                for z in planes:
                    if z in path:
                        plane(z, unit, path[z], onward, arriving)
                        arriving = {x: (onward,) for x in path[z]}
                for x, kinds in arriving.items():
                    merged[x] = merged.get(x, ()) + kinds
            plane(home, unit, (column,), KEEP, merged)
    return steps


def stream_words(depth, panels, per_tile):
    steps = device_steps(depth, panels)

    def target(device, way):
        z, x = device
        return {CROSS: (z, 1 - x), UP: (z + 1, x), DOWN: (z - 1, x)}[way]

    bases, sent = {}, {}
    for device, streams in PLAN.items():
        for way in (CROSS, UP, DOWN):
            base = 0
            for _, unit in streams[way]:
                assert steps[device][unit][2] == way
                bases[target(device, way), unit, way] = base
                base += pieces(unit, per_tile)[1]
            sent[device, way] = base
    words, leads = {}, {}
    for device, streams in PLAN.items():
        planned = [unit for stream in streams for _, unit in stream]
        assert sorted(planned) == sorted(steps[device])
        origin, words[device] = panels * (PAIR * device[0] + device[1]), []
        for way, stream in enumerate(streams):
            line, free = [], 0
            for start, unit in stream:
                own, arriving, onward = steps[device][unit]
                begin, length = pieces(unit, per_tile)
                start = start * per_tile // 8
                assert onward == way and start >= free
                free = start + length
                base = 0 if way == KEEP else bases[target(device, way), unit, way]
                one = (unit // 2 - origin) % SITE_TILES + 16 * begin + 128 * base
                two = sum((1 + 2 * bases[device, unit, kind]) * 128**kind for kind in arriving)
                line.append((start, length, one, two))
            words[device].append(line)
        for way in (CROSS, UP, DOWN):
            start, unit = (streams[way] or [(2**20, 0)])[0]
            own, arriving, _ = steps[device].get(unit, (False, (), way))
            leads[device, way] = own and not arriving and start <= LEAD
            assert not leads[device, way] or pieces(unit, per_tile)[0] == pieces(streams[CROSS][0][1], per_tile)[0]
    return words, sent, leads


def field_kernel(
    words, sent, leads, own_reals, rows_in, eps_in, factor_in, median_in, spread_in, critical_in, field, mean_out,
    block_rows, sites_in, eps, factor, head, x_out, u_out, d_out, x_in, u_in, d_in, spare, totals, columns, folds, table,
    load_sem, site_sem, x_send, u_send, d_send, x_recv, u_recv, d_recv, t_send, t_recv,
):
    panels, per_column, tile = factor.shape[0], factor.shape[1], factor.shape[2]
    depth = len(words) // PAIR
    count = PAIR * depth
    per_tile = tile // ROWS
    lines = panels * tile // LANES
    reals = lax.axis_size("real")
    site = lax.axis_index("site")
    me = lax.axis_index("real")
    z, x = site // PAIR, site % PAIR
    here = {device: site == device[0] * PAIR + device[1] for device in words}

    def pick(values):
        result = None
        for device, value in values.items():
            value = jnp.int32(value)
            result = value if result is None else jnp.where(here[device], value, result)
        return result

    barrier = pltpu.get_barrier_semaphore()
    pl.semaphore_signal(barrier, inc=1, device_id={"site": site + 1 - 2 * x}, device_id_type=MESH)
    for shift in range(1, reals):
        pl.semaphore_signal(barrier, inc=1, device_id={"real": (me + shift) % reals}, device_id_type=MESH)

    @pl.when(z > 0)
    def _():
        pl.semaphore_signal(barrier, inc=1, device_id={"site": site - PAIR}, device_id_type=MESH)

    @pl.when(z < depth - 1)
    def _():
        pl.semaphore_signal(barrier, inc=1, device_id={"site": site + PAIR}, device_id_type=MESH)

    begin = pick({device: own[CROSS][0][2] // 16 % 8 * ROWS for device, own in words.items()})
    first = [pltpu.make_async_copy(eps_in, eps, load_sem.at[0])]
    rest = []
    for panel in range(panels):
        first.append(pltpu.make_async_copy(
            factor_in.at[panel, :, pl.ds(pl.multiple_of(begin, ROWS), head.shape[2]), :],
            head.at[panel], load_sem.at[1 + panel],
        ))
        rest.append(pltpu.make_async_copy(
            factor_in.at[panel], factor.at[panel], load_sem.at[1 + panels + panel]
        ))
    known = [pltpu.make_async_copy(rows_in, block_rows, site_sem.at[0])]
    for index, ref in enumerate((median_in, spread_in, critical_in)):
        known.append(pltpu.make_async_copy(ref, sites_in.at[index], site_sem.at[1 + index]))
    for load in known + first + rest:
        load.start()

    plan, slots = [], 0
    for way in range(4):
        longest = max(len(own[way]) for own in words.values())
        pad = [(2**20, 0, 0, 0)] * longest
        plan.append([
            [pick({device: (own[way] + pad)[number][field] for device, own in words.items()}) for field in range(4)]
            for number in range(longest)
        ])
        slots = max([slots] + [own[way][-1][0] + own[way][-1][1] for own in words.values() if own[way]])

    for load in known:
        load.wait()
    for panel in range(panels):
        begins = [
            (block_rows[panel, block] - site * panels + panels * count) % (panels * count)
            for block in range(per_column)
        ]

        @pl.loop(0, table.shape[1])
        def _(slot):
            number, found = jnp.int32(0), jnp.int32(0)
            for block in range(per_column):
                hit = begins[block] == slot
                number = jnp.where(hit, block, number)
                found = jnp.where(hit, 1, found)
            table[panel, slot] = number
            table[panels + panel, slot] = found

    def bits(word, low, width):
        return lax.rem(lax.div(word, jnp.int32(2**low)), jnp.int32(2**width))

    def multiply(out, relative, piece, source):
        @pl.when(relative <= LAST_OFFSET)
        def _():
            row = pl.multiple_of(piece * ROWS, ROWS)
            blocks = [
                source[panel, table[panel, relative], pl.ds(row, ROWS), :]
                * table[panels + panel, relative].astype(jnp.float32).astype(source.dtype)
                for panel in range(panels)
            ]
            result = jnp.dot(jnp.concatenate(blocks, axis=1), eps[...], preferred_element_type=jnp.float32)
            out[...] = result

        @pl.when(relative > LAST_OFFSET)
        def _():
            out[...] = jnp.zeros_like(out)

    ways = (
        (x_out, x_in, x_send, x_recv, site + 1 - 2 * x),
        (u_out, u_in, u_send, u_recv, (site + PAIR) % count),
        (d_out, d_in, d_send, d_recv, (site + count - PAIR) % count),
    )

    def copy(way, slot):
        leaving, landing, departure, arrival, there = ways[way]
        return pltpu.make_async_remote_copy(
            src_ref=leaving.at[slot],
            dst_ref=landing.at[slot],
            send_sem=departure.at[slot],
            recv_sem=arrival.at[slot],
            device_id={"site": there},
            device_id_type=MESH,
        )

    def keep(chunk):
        rounded = spare[...].astype(jnp.bfloat16)
        rows = pl.ds(pl.multiple_of(chunk * ROWS, ROWS), ROWS)
        field[rows, :] = rounded
        folded = None
        for piece in range(own_reals // LANES):
            residual = rounded[:, piece * LANES:(piece + 1) * LANES].astype(jnp.float32)
            log_peak = columns[0, rows, :] + columns[1, rows, :] * residual
            log_ratio = columns[2, rows, :] - log_peak
            margin = jnp.maximum(1.0 - jnp.exp(log_ratio), 0.0)
            displacement = coeff_disp * jnp.exp(power_margin * jnp.log(margin) - power_ratio * log_ratio)
            damage = jnp.log1p(displacement)
            folded = damage if folded is None else folded + damage
        folds[rows, :] = folded

        @pl.when((chunk + 1) % (LANES // ROWS) == 0)
        def _():
            line = chunk // (LANES // ROWS)
            group = folds[pl.ds(pl.multiple_of(line * LANES, LANES), LANES), :]
            totals[me, pl.ds(line, 1), :] = jnp.sum(group.T, axis=0, keepdims=True)

    def step(way, slot, least=0):
        turn, count, one, two = jnp.int32(0), jnp.int32(0), jnp.int32(0), jnp.int32(0)
        for start, length, first_word, second_word in plan[way]:
            later = slot >= start
            turn = jnp.where(later, slot - start, turn)
            count = jnp.where(later, length, count)
            one = jnp.where(later, first_word, one)
            two = jnp.where(later, second_word, two)

        @pl.when(jnp.logical_and(turn < count, slot >= least))
        def _():
            relative = bits(one, 0, 4)
            piece = bits(one, 4, 3) + turn
            place = bits(one, 7, 6) + turn
            out = spare if way == KEEP else ways[way][0].at[place]
            multiply(out, relative, piece, factor)
            for kind in range(3):
                @pl.when(bits(two, 7 * kind, 1) == 1)
                def _():
                    arrived = bits(two, 7 * kind + 1, 6) + turn
                    copy(kind, arrived).wait_recv()
                    out[...] = out[...] + ways[kind][1][arrived]

            if way == KEEP:
                keep(relative * per_tile + piece)
            else:
                copy(way, place).start()

    for load in first:
        load.wait()
    ahead = [pick({device: leads[device, way] for device in words}) for way in (CROSS, UP, DOWN)]
    for turn in range(HEAD):
        for way in (CROSS, UP, DOWN):
            @pl.when(ahead[way] == 1)
            def _():
                multiply(ways[way][0].at[turn], bits(plan[way][0][2], 0, 4), turn, head)

        if turn == 0:
            pl.semaphore_wait(barrier, reals + jnp.where(z > 0, 1, 0) + jnp.where(z < depth - 1, 1, 0))

        for way in (CROSS, UP, DOWN):
            @pl.when(ahead[way] == 1)
            def _():
                copy(way, turn).start()

    for load in rest:
        load.wait()

    @pl.loop(0, slots)
    def _(slot):
        step(CROSS, slot, plan[CROSS][0][0] + HEAD * ahead[CROSS])

        @pl.when(slot < lines)
        def _():
            spot = pl.ds(pl.multiple_of(slot * LANES, LANES), LANES)
            for index in range(3):
                value = sites_in[index, pl.ds(slot, 1), :]
                value = jnp.log(value) if index == 2 else value
                columns[index, spot, :] = jnp.broadcast_to(value, (LANES, LANES)).T

        for way in (UP, DOWN):
            step(way, slot, plan[way][0][0] + HEAD * ahead[way])
        step(KEEP, slot)

    def t_copy(shift):
        return pltpu.make_async_remote_copy(
            src_ref=totals.at[me],
            dst_ref=totals.at[me],
            send_sem=t_send.at[shift],
            recv_sem=t_recv.at[shift],
            device_id={"real": (me + shift) % reals},
            device_id_type=MESH,
        )

    for shift in range(1, reals):
        t_copy(shift).start()

    for way in (CROSS, UP, DOWN):
        @pl.loop(0, pick({device: sent[device, way] for device in words}))
        def _(slot):
            copy(way, slot).wait_send()

    for shift in range(1, reals):
        t_copy(shift).wait()
    total = totals[0]
    for source in range(1, reals):
        total = total + totals[source]
    mean_out[...] = total / (own_reals * reals)


def hand_out_kernel(field, mean, field_out, mean_out, out_sem):
    part = field.shape[0] // PARTS
    writes = [pltpu.make_async_copy(mean, mean_out, out_sem.at[PARTS])]
    for index in range(PARTS):
        rows = pl.ds(index * part, part)
        writes.append(pltpu.make_async_copy(field.at[rows, :], field_out.at[rows, :], out_sem.at[index]))
    for write in writes:
        write.start()
    for write in writes:
        write.wait()


def line_shards(epsilon, factor, block_rows, median_log, spread_log, critical_yield):
    panels, per_column, tile = factor.shape[:3]
    sites, own_reals = epsilon.shape
    count, reals = lax.axis_size("site"), lax.axis_size("real")
    lines = sites // LANES
    words, sent, leads = stream_words(count // PAIR, panels, tile // ROWS)
    most = [max(sent[device, way] for device in words) for way in (CROSS, UP, DOWN)]
    piece = (ROWS, own_reals)
    vmem = pl.BlockSpec(memory_space=pltpu.VMEM)
    anywhere = pl.BlockSpec(memory_space=pl.ANY)
    field, mean = pl.pallas_call(
        functools.partial(field_kernel, words, sent, leads, own_reals),
        out_shape=(
            pltpu.VMEM((sites, own_reals), jnp.bfloat16),
            pltpu.VMEM((lines, LANES), jnp.float32),
        ),
        in_specs=[anywhere] * 6,
        out_specs=(vmem, vmem),
        scratch_shapes=[
            pltpu.SMEM(block_rows.shape, block_rows.dtype),
            pltpu.VMEM((3, lines, LANES), jnp.float32),
            pltpu.VMEM(epsilon.shape, epsilon.dtype),
            pltpu.VMEM(factor.shape, factor.dtype),
            pltpu.VMEM((panels, per_column, HEAD * ROWS, tile), factor.dtype),
            *[pltpu.VMEM((slots,) + piece, jnp.float32) for slots in most + most],
            pltpu.VMEM(piece, jnp.float32),
            pltpu.VMEM((reals, lines, LANES), jnp.float32),
            pltpu.VMEM((3, sites, LANES), jnp.float32),
            pltpu.VMEM((sites, LANES), jnp.float32),
            pltpu.SMEM((2 * panels, SITE_TILES), jnp.int32),
            pltpu.SemaphoreType.DMA((1 + 2 * panels,)),
            pltpu.SemaphoreType.DMA((4,)),
            *[pltpu.SemaphoreType.DMA((slots,)) for slots in most + most],
            pltpu.SemaphoreType.DMA((reals,)),
            pltpu.SemaphoreType.DMA((reals,)),
        ],
        compiler_params=pltpu.CompilerParams(
            collective_id=0, has_side_effects=True, vmem_limit_bytes=60 * 1024 * 1024
        ),
    )(
        block_rows,
        epsilon,
        factor,
        median_log.reshape(lines, LANES),
        spread_log.reshape(lines, LANES),
        critical_yield.reshape(lines, LANES),
    )
    field, mean = pl.pallas_call(
        hand_out_kernel,
        out_shape=(
            jax.ShapeDtypeStruct(field.shape, field.dtype),
            jax.ShapeDtypeStruct(mean.shape, mean.dtype),
        ),
        in_specs=[vmem, vmem],
        out_specs=(anywhere, anywhere),
        scratch_shapes=[pltpu.SemaphoreType.DMA((PARTS + 1,))],
    )(pltpu.with_memory_space_constraint(field, pltpu.VMEM), pltpu.with_memory_space_constraint(mean, pltpu.VMEM))
    return field, mean.reshape(sites)


def solution(mesh):
    body = line_shards if mesh.shape["site"] == BAND // 2 + PAIR else shards
    return jax.shard_map(
        body,
        mesh=mesh,
        in_specs=(
            P("site", "real"),
            P(None, "site", None, None),
            P(None, "site"),
            P("site"),
            P("site"),
            P("site"),
        ),
        out_specs=(P("site", "real"), P("site")),
        check_vma=False,
    )
```

```python
import functools
import jax
import jax.numpy as jnp
from jax import lax
from jax.experimental import pallas as pl
from jax.experimental.pallas import tpu as pltpu
from jax.sharding import PartitionSpec as P

BAND = 12
PAIR = 2
LANES = 128
ROWS = 64
PARTS = 4
HEAD = 2
LEAD = 3
SITE_TILES = 16
LAST_OFFSET = 12
CROSS, UP, DOWN, KEEP = range(4)
MESH = pl.DeviceIdType.MESH

coeff_disp = 10.0**0.215
power_margin = 2.341
power_ratio = 1.438


def passed_along(value, axis, steps):
    count = lax.axis_size(axis)
    pairs = [(source, (source + steps) % count) for source in range(count)]
    return lax.ppermute(value, axis, pairs)


def shards(epsilon, factor, block_rows, median_log, spread_log, critical_yield):
    panels = factor.shape[0]
    per_column = factor.shape[1]
    tile_size = factor.shape[-1]
    own_reals = epsilon.shape[1]
    reach = BAND // 2
    own_index = lax.axis_index("site")
    total_tiles = panels * lax.axis_size("site")
    draws = epsilon.reshape(panels, tile_size, own_reals)

    def pending(panel):
        flat = factor[panel].reshape(per_column * tile_size, tile_size)
        products = jnp.dot(flat, draws[panel], preferred_element_type=jnp.float32)
        products = products.reshape(per_column, tile_size, own_reals)
        relative = (block_rows[panel] - own_index * panels) % total_tiles
        slots = jnp.zeros(((reach + 1) * panels, tile_size, own_reals), jnp.float32)
        sums = slots.at[relative].set(products, unique_indices=True)
        return sums.reshape(reach + 1, panels, tile_size, own_reals)

    combined = pending(0)
    panel = 1
    combined = combined + pending(panel)
    arrived = combined[0]
    for offset in range(1, reach + 1):
        arrived = arrived + passed_along(combined[offset], "site", offset)
    residual_field = arrived.astype(jnp.bfloat16).reshape(panels * tile_size, own_reals)
    log_peak = median_log[:, None] + spread_log[:, None] * residual_field.astype(jnp.float32)
    log_ratio = jnp.log(critical_yield)[:, None] - log_peak
    ratio = jnp.exp(log_ratio)
    margin = jnp.maximum(1.0 - ratio, 0.0)
    displacement = coeff_disp * jnp.power(margin, power_margin) * jnp.exp(-power_ratio * log_ratio)
    local_total = jnp.sum(jnp.log1p(displacement), axis=1)
    total = lax.psum(local_total, "real")
    mean_damage = total / (own_reals * lax.axis_size("real"))
    return (residual_field, mean_damage)

LEFT, RIGHT, BOTH = (0,), (1,), (0, 1)
ROUTES = {
    0: [({}, {3: LEFT, 2: BOTH, 1: LEFT})] * 2,
    1: [({}, {3: LEFT, 2: BOTH, 1: LEFT})] * 2,
    2: [({}, {3: RIGHT, 2: RIGHT, 1: RIGHT})] * 2,
    3: [({}, {3: RIGHT, 2: RIGHT, 1: RIGHT})] * 2,
    4: [({0: LEFT}, {3: LEFT, 2: LEFT})] * 2,
    5: [({0: LEFT}, {3: LEFT, 2: LEFT})] * 2,
    6: [({0: RIGHT}, {3: RIGHT, 2: RIGHT})] * 2,
    7: [({0: LEFT}, {3: LEFT, 2: LEFT}), ({0: RIGHT}, {3: RIGHT, 2: RIGHT})],
    8: [({0: LEFT, 1: LEFT}, {3: LEFT})] * 2,
    9: [({0: LEFT, 1: BOTH}, {3: RIGHT})] * 2,
    10: [({0: RIGHT, 1: RIGHT}, {3: RIGHT})] * 2,
    11: [({0: RIGHT, 1: RIGHT}, {})] * 2,
    12: [({0: LEFT, 1: LEFT, 2: LEFT}, {})] * 2,
    13: [({0: RIGHT, 1: LEFT, 2: LEFT}, {})] * 2,
    14: [({0: RIGHT, 1: RIGHT, 2: RIGHT}, {})] * 2,
    15: [({1: BOTH, 2: BOTH}, {})] * 2,
}

SPLITS = {7: 3}

PLAN = {
    (0, 0): (
        [(0, 20, 0), (4, 22, 0), (10, 21, 0), (15, 15, 0), (20, 23, 0), (27, 5, 0), (36, 12, 0), (42, 13, 0), (46, 7, 0), (50, 4, 0), (54, 6, 0)],
        [(4, 25, 0), (8, 10, 0), (15, 18, 0), (20, 19, 0), (27, 24, 0), (35, 14, 0), (38, 11, 0), (43, 8, 0), (47, 17, 0), (51, 16, 0), (55, 9, 0)],
        [],
        [(33, 0, 0), (42, 2, 0), (51, 1, 0), (55, 3, 0)],
    ),
    (0, 1): (
        [(0, 25, 0), (4, 10, 0), (8, 18, 0), (12, 19, 0), (20, 24, 0), (28, 14, 0), (31, 11, 0), (35, 8, 0), (39, 17, 0), (43, 16, 0), (47, 9, 0)],
        [(2, 27, 0), (6, 26, 1), (15, 29, 1), (19, 28, 1), (26, 22, 1), (30, 23, 1), (34, 21, 1), (38, 12, 0), (42, 20, 0), (46, 13, 0), (51, 15, 0)],
        [],
        [(39, 5, 0), (46, 7, 0), (51, 4, 0), (56, 6, 0)],
    ),
    (1, 0): (
        [(3, 28, 0), (7, 22, 0), (11, 20, 0), (17, 23, 0), (23, 12, 0), (30, 29, 0), (35, 21, 0), (45, 14, 0), (48, 13, 0), (52, 15, 0)],
        [(0, 30, 0), (6, 31, 0), (12, 26, 0), (17, 27, 0), (21, 19, 0), (29, 18, 0), (36, 24, 0), (42, 25, 0), (49, 17, 0), (54, 16, 0)],
        [(18, 0, 0), (35, 2, 0), (44, 1, 0), (54, 3, 0)],
        [(37, 11, 0), (44, 8, 0), (48, 10, 0), (56, 9, 0)],
    ),
    (1, 1): (
        [(2, 24, 0), (8, 27, 0), (12, 26, 0), (16, 0, 0), (20, 25, 0), (24, 2, 0), (28, 16, 0), (32, 1, 0), (39, 17, 0), (48, 3, 0)],
        [(1, 30, 0), (5, 19, 0), (13, 18, 0), (18, 31, 0), (25, 28, 0), (32, 23, 0), (36, 29, 0), (40, 22, 0), (46, 20, 0), (53, 21, 0)],
        [(30, 5, 0), (35, 7, 0), (42, 6, 0), (50, 4, 0)],
        [(42, 12, 0), (47, 14, 0), (50, 13, 0), (54, 15, 0)],
    ),
    (2, 0): (
        [(0, 7, 0), (4, 28, 0), (9, 6, 0), (13, 22, 0), (18, 5, 0), (24, 23, 0), (29, 29, 0), (36, 4, 0), (46, 20, 0), (52, 21, 0)],
        [(10, 31, 0), (14, 30, 0), (22, 27, 0), (37, 26, 0), (48, 25, 0), (54, 24, 0)],
        [(8, 0, 0), (12, 11, 0), (18, 14, 0), (21, 1, 0), (27, 2, 0), (37, 8, 0), (43, 10, 0), (50, 3, 0), (54, 9, 0)],
        [(47, 19, 0), (51, 18, 0), (55, 17, 0), (59, 16, 0)],
    ),
    (2, 1): (
        [(0, 27, 0), (4, 11, 0), (8, 25, 0), (12, 8, 0), (19, 10, 0), (28, 24, 0), (34, 26, 0), (40, 19, 0), (49, 18, 0), (53, 9, 0)],
        [(5, 30, 0), (32, 28, 0), (36, 31, 0), (44, 29, 0)],
        [(0, 1, 0), (4, 2, 0), (8, 0, 0), (13, 6, 0), (20, 3, 0), (29, 5, 0), (33, 7, 0), (38, 12, 0), (42, 13, 0), (48, 4, 0), (52, 15, 0)],
        [(40, 23, 0), (48, 22, 0), (52, 20, 0), (56, 21, 0)],
    ),
    (3, 0): (
        [(0, 5, 0), (4, 6, 0), (8, 12, 0), (14, 31, 0), (21, 7, 0), (27, 13, 0), (31, 15, 0), (38, 4, 0), (42, 28, 0), (46, 29, 0), (52, 30, 0)],
        [],
        [(2, 0, 0), (6, 11, 0), (13, 1, 0), (21, 14, 0), (26, 2, 0), (32, 10, 0), (37, 8, 0), (41, 9, 0), (45, 3, 0), (49, 17, 0), (53, 16, 0)],
        [(43, 26, 0), (47, 27, 0), (51, 25, 0), (55, 24, 0)],
    ),
    (3, 1): (
        [(0, 0, 0), (4, 11, 0), (10, 1, 0), (14, 14, 0), (17, 2, 0), (21, 10, 0), (27, 8, 0), (31, 9, 0), (38, 3, 0), (44, 17, 0), (48, 16, 0)],
        [],
        [(0, 18, 0), (4, 19, 1), (8, 6, 1), (12, 20, 1), (22, 5, 1), (26, 7, 1), (30, 12, 1), (34, 13, 1), (39, 4, 0), (44, 15, 0), (54, 21, 0)],
        [(37, 31, 0), (44, 28, 0), (52, 29, 0), (56, 30, 0)],
    ),
}


def pieces(unit, per_tile):
    cut = SPLITS.get(unit // 2, 4) * per_tile // 8
    return (cut, per_tile - cut) if unit % 2 else (0, cut)


def device_steps(depth, panels):
    steps = {(z, x): {} for z in range(depth) for x in range(PAIR)}

    def plane(z, unit, leaves, onward, arriving):
        own = [(unit // 2 - panels * (PAIR * z + x)) % SITE_TILES <= LAST_OFFSET for x in range(PAIR)]
        held = [x for x in range(PAIR) if own[x] or arriving.get(x)]
        for x in held:
            if x not in leaves:
                steps[z, x][unit] = (own[x], tuple(arriving.get(x, ())), CROSS)
        crossed = (CROSS,) if any(x not in leaves for x in held) else ()
        for x in leaves:
            steps[z, x][unit] = (own[x], tuple(arriving.get(x, ())) + crossed, onward)

    for row, halves in ROUTES.items():
        home, column = row // (panels * PAIR), row // panels % PAIR
        for half, (rising, falling) in enumerate(halves):
            unit, merged = 2 * row + half, {}
            for onward, path, planes in ((UP, rising, range(home)), (DOWN, falling, range(depth - 1, home, -1))):
                arriving = {}
                for z in planes:
                    if z in path:
                        plane(z, unit, path[z], onward, arriving)
                        arriving = {x: (onward,) for x in path[z]}
                for x, kinds in arriving.items():
                    merged[x] = merged.get(x, ()) + kinds
            plane(home, unit, (column,), KEEP, merged)
    return steps


def stream_words(depth, panels, per_tile):
    steps = device_steps(depth, panels)

    def target(device, way):
        z, x = device
        return {CROSS: (z, 1 - x), UP: (z + 1, x), DOWN: (z - 1, x)}[way]

    bases, paired, sent = {}, {}, {}
    for device, streams in PLAN.items():
        for way in (CROSS, UP, DOWN):
            base = 0
            for number, (_, unit, pairs) in enumerate(streams[way]):
                assert steps[device][unit][2] == way
                assert not pairs or (number and pieces(unit, per_tile)[1] % 2 == 0)
                paired[target(device, way), unit, way] = pairs
                bases[target(device, way), unit, way] = base
                base += pieces(unit, per_tile)[1]
            sent[device, way] = base
    words, leads = {}, {}
    for device, streams in PLAN.items():
        planned = [unit for stream in streams for _, unit, _ in stream]
        assert sorted(planned) == sorted(steps[device])
        origin, words[device] = panels * (PAIR * device[0] + device[1]), []
        for way, stream in enumerate(streams):
            line, free = [], 0
            for start, unit, pairs in stream:
                own, arriving, onward = steps[device][unit]
                begin, length = pieces(unit, per_tile)
                start = start * per_tile // 8
                assert onward == way and start >= free
                free = start + length
                base = 0 if way == KEEP else bases[target(device, way), unit, way]
                one = (unit // 2 - origin) % SITE_TILES + 16 * begin + 128 * base + 8192 * pairs
                two = sum(
                    (1 + 2 * bases[device, unit, kind] + 128 * paired[device, unit, kind]) * 256**kind for kind in arriving
                )
                line.append((start, length, one, two))
            words[device].append(line)
        for way in (CROSS, UP, DOWN):
            start, unit, _ = (streams[way] or [(2**20, 0, 0)])[0]
            own, arriving, _ = steps[device].get(unit, (False, (), way))
            leads[device, way] = own and not arriving and start <= LEAD
            assert not leads[device, way] or pieces(unit, per_tile)[0] == pieces(streams[CROSS][0][1], per_tile)[0]
    return words, sent, leads


def field_kernel(
    words, sent, leads, own_reals, rows_in, eps_in, factor_in, median_in, spread_in, critical_in, field, mean_out,
    block_rows, sites_in, eps, factor, head, x_out, u_out, d_out, x_in, u_in, d_in, spare, totals, columns, folds, table,
    load_sem, site_sem, x_send, u_send, d_send, x_recv, u_recv, d_recv, t_send, t_recv,
):
    panels, per_column, tile = factor.shape[0], factor.shape[1], factor.shape[2]
    depth = len(words) // PAIR
    count = PAIR * depth
    per_tile = tile // ROWS
    lines = panels * tile // LANES
    reals = lax.axis_size("real")
    site = lax.axis_index("site")
    me = lax.axis_index("real")
    z, x = site // PAIR, site % PAIR
    here = {device: site == device[0] * PAIR + device[1] for device in words}

    def pick(values):
        result = None
        for device, value in values.items():
            value = jnp.int32(value)
            result = value if result is None else jnp.where(here[device], value, result)
        return result

    barrier = pltpu.get_barrier_semaphore()
    pl.semaphore_signal(barrier, inc=1, device_id={"site": site + 1 - 2 * x}, device_id_type=MESH)
    for shift in range(1, reals):
        pl.semaphore_signal(barrier, inc=1, device_id={"real": (me + shift) % reals}, device_id_type=MESH)

    @pl.when(z > 0)
    def _():
        pl.semaphore_signal(barrier, inc=1, device_id={"site": site - PAIR}, device_id_type=MESH)

    @pl.when(z < depth - 1)
    def _():
        pl.semaphore_signal(barrier, inc=1, device_id={"site": site + PAIR}, device_id_type=MESH)

    begin = pick({device: own[CROSS][0][2] // 16 % 8 * ROWS for device, own in words.items()})
    first = [pltpu.make_async_copy(eps_in, eps, load_sem.at[0])]
    rest = []
    for panel in range(panels):
        first.append(pltpu.make_async_copy(
            factor_in.at[panel, :, pl.ds(pl.multiple_of(begin, ROWS), head.shape[2]), :],
            head.at[panel], load_sem.at[1 + panel],
        ))
        rest.append(pltpu.make_async_copy(
            factor_in.at[panel], factor.at[panel], load_sem.at[1 + panels + panel]
        ))
    known = [pltpu.make_async_copy(rows_in, block_rows, site_sem.at[0])]
    for index, ref in enumerate((median_in, spread_in, critical_in)):
        known.append(pltpu.make_async_copy(ref, sites_in.at[index], site_sem.at[1 + index]))
    for load in known + first + rest:
        load.start()

    plan, slots = [], 0
    for way in range(4):
        longest = max(len(own[way]) for own in words.values())
        pad = [(2**20, 0, 0, 0)] * longest
        plan.append([
            [pick({device: (own[way] + pad)[number][field] for device, own in words.items()}) for field in range(4)]
            for number in range(longest)
        ])
        slots = max([slots] + [own[way][-1][0] + own[way][-1][1] for own in words.values() if own[way]])

    for load in known:
        load.wait()
    for panel in range(panels):
        begins = [
            (block_rows[panel, block] - site * panels + panels * count) % (panels * count)
            for block in range(per_column)
        ]

        @pl.loop(0, table.shape[1])
        def _(slot):
            number, found = jnp.int32(0), jnp.int32(0)
            for block in range(per_column):
                hit = begins[block] == slot
                number = jnp.where(hit, block, number)
                found = jnp.where(hit, 1, found)
            table[panel, slot] = number
            table[panels + panel, slot] = found

    def bits(word, low, width):
        return lax.rem(lax.div(word, jnp.int32(2**low)), jnp.int32(2**width))

    def multiply(out, relative, piece, source):
        @pl.when(relative <= LAST_OFFSET)
        def _():
            row = pl.multiple_of(piece * ROWS, ROWS)
            blocks = [
                source[panel, table[panel, relative], pl.ds(row, ROWS), :]
                * table[panels + panel, relative].astype(jnp.float32).astype(source.dtype)
                for panel in range(panels)
            ]
            result = jnp.dot(jnp.concatenate(blocks, axis=1), eps[...], preferred_element_type=jnp.float32)
            out[...] = result

        @pl.when(relative > LAST_OFFSET)
        def _():
            out[...] = jnp.zeros_like(out)

    ways = (
        (x_out, x_in, x_send, x_recv, site + 1 - 2 * x),
        (u_out, u_in, u_send, u_recv, (site + PAIR) % count),
        (d_out, d_in, d_send, d_recv, (site + count - PAIR) % count),
    )

    def copy(way, slot, extent=1):
        leaving, landing, departure, arrival, there = ways[way]
        return pltpu.make_async_remote_copy(
            src_ref=leaving.at[pl.ds(slot, extent)],
            dst_ref=landing.at[pl.ds(slot, extent)],
            send_sem=departure.at[slot],
            recv_sem=arrival.at[slot],
            device_id={"site": there},
            device_id_type=MESH,
        )

    def keep(chunk):
        rounded = spare[...].astype(jnp.bfloat16)
        rows = pl.ds(pl.multiple_of(chunk * ROWS, ROWS), ROWS)
        field[rows, :] = rounded
        folded = None
        for piece in range(own_reals // LANES):
            residual = rounded[:, piece * LANES:(piece + 1) * LANES].astype(jnp.float32)
            log_peak = columns[0, rows, :] + columns[1, rows, :] * residual
            log_ratio = columns[2, rows, :] - log_peak
            margin = jnp.maximum(1.0 - jnp.exp(log_ratio), 0.0)
            displacement = coeff_disp * jnp.exp(power_margin * jnp.log(margin) - power_ratio * log_ratio)
            damage = jnp.log1p(displacement)
            folded = damage if folded is None else folded + damage
        folds[rows, :] = folded

        @pl.when((chunk + 1) % (LANES // ROWS) == 0)
        def _():
            line = chunk // (LANES // ROWS)
            group = folds[pl.ds(pl.multiple_of(line * LANES, LANES), LANES), :]
            totals[me, pl.ds(line, 1), :] = jnp.sum(group.T, axis=0, keepdims=True)

    def step(way, slot, least=0):
        turn, count, one, two = jnp.int32(0), jnp.int32(0), jnp.int32(0), jnp.int32(0)
        for start, length, first_word, second_word in plan[way]:
            later = slot >= start
            turn = jnp.where(later, slot - start, turn)
            count = jnp.where(later, length, count)
            one = jnp.where(later, first_word, one)
            two = jnp.where(later, second_word, two)

        @pl.when(jnp.logical_and(turn < count, slot >= least))
        def _():
            relative = bits(one, 0, 4)
            piece = bits(one, 4, 3) + turn
            place = bits(one, 7, 6) + turn
            out = spare if way == KEEP else ways[way][0].at[place]
            multiply(out, relative, piece, factor)
            for kind in range(3):
                @pl.when(bits(two, 8 * kind, 1) == 1)
                def _():
                    arrived = bits(two, 8 * kind + 1, 6) + turn
                    of_pair = bits(two, 8 * kind + 7, 1)

                    @pl.when(of_pair == 0)
                    def _():
                        copy(kind, arrived).wait_recv()

                    @pl.when(jnp.logical_and(of_pair == 1, turn % 2 == 0))
                    def _():
                        copy(kind, arrived, 2).wait_recv()

                    out[...] = out[...] + ways[kind][1][arrived]

            if way == KEEP:
                keep(relative * per_tile + piece)
                return

            @pl.when(bits(one, 13, 1) == 0)
            def _():
                copy(way, place).start()

            @pl.when(jnp.logical_and(bits(one, 13, 1) == 1, turn % 2 == 1))
            def _():
                copy(way, place - 1, 2).start()

    for load in first:
        load.wait()
    ahead = [pick({device: leads[device, way] for device in words}) for way in (CROSS, UP, DOWN)]
    for turn in range(HEAD):
        for way in (CROSS, UP, DOWN):
            @pl.when(ahead[way] == 1)
            def _():
                multiply(ways[way][0].at[turn], bits(plan[way][0][2], 0, 4), turn, head)

        if turn == 0:
            pl.semaphore_wait(barrier, reals + jnp.where(z > 0, 1, 0) + jnp.where(z < depth - 1, 1, 0))

        for way in (CROSS, UP, DOWN):
            @pl.when(ahead[way] == 1)
            def _():
                copy(way, turn).start()

    for load in rest:
        load.wait()

    @pl.loop(0, slots)
    def _(slot):
        step(CROSS, slot, plan[CROSS][0][0] + HEAD * ahead[CROSS])

        @pl.when(slot < lines)
        def _():
            spot = pl.ds(pl.multiple_of(slot * LANES, LANES), LANES)
            for index in range(3):
                value = sites_in[index, pl.ds(slot, 1), :]
                value = jnp.log(value) if index == 2 else value
                columns[index, spot, :] = jnp.broadcast_to(value, (LANES, LANES)).T

        for way in (UP, DOWN):
            step(way, slot, plan[way][0][0] + HEAD * ahead[way])
        step(KEEP, slot)

    def t_copy(shift):
        return pltpu.make_async_remote_copy(
            src_ref=totals.at[me],
            dst_ref=totals.at[me],
            send_sem=t_send.at[shift],
            recv_sem=t_recv.at[shift],
            device_id={"real": (me + shift) % reals},
            device_id_type=MESH,
        )

    for shift in range(1, reals):
        t_copy(shift).start()

    for way in (CROSS, UP, DOWN):
        for _, length, one, _ in plan[way]:
            @pl.loop(0, length)
            def _(turn):
                place = bits(one, 7, 6) + turn

                @pl.when(bits(one, 13, 1) == 0)
                def _():
                    copy(way, place).wait_send()

                @pl.when(jnp.logical_and(bits(one, 13, 1) == 1, turn % 2 == 0))
                def _():
                    copy(way, place, 2).wait_send()

    for shift in range(1, reals):
        t_copy(shift).wait()
    total = totals[0]
    for source in range(1, reals):
        total = total + totals[source]
    mean_out[...] = total / (own_reals * reals)


def hand_out_kernel(field, mean, field_out, mean_out, out_sem):
    part = field.shape[0] // PARTS
    writes = [pltpu.make_async_copy(mean, mean_out, out_sem.at[PARTS])]
    for index in range(PARTS):
        rows = pl.ds(index * part, part)
        writes.append(pltpu.make_async_copy(field.at[rows, :], field_out.at[rows, :], out_sem.at[index]))
    for write in writes:
        write.start()
    for write in writes:
        write.wait()


def line_shards(epsilon, factor, block_rows, median_log, spread_log, critical_yield):
    panels, per_column, tile = factor.shape[:3]
    sites, own_reals = epsilon.shape
    count, reals = lax.axis_size("site"), lax.axis_size("real")
    lines = sites // LANES
    words, sent, leads = stream_words(count // PAIR, panels, tile // ROWS)
    most = [max(sent[device, way] for device in words) for way in (CROSS, UP, DOWN)]
    piece = (ROWS, own_reals)
    vmem = pl.BlockSpec(memory_space=pltpu.VMEM)
    anywhere = pl.BlockSpec(memory_space=pl.ANY)
    field, mean = pl.pallas_call(
        functools.partial(field_kernel, words, sent, leads, own_reals),
        out_shape=(
            pltpu.VMEM((sites, own_reals), jnp.bfloat16),
            pltpu.VMEM((lines, LANES), jnp.float32),
        ),
        in_specs=[anywhere] * 6,
        out_specs=(vmem, vmem),
        scratch_shapes=[
            pltpu.SMEM(block_rows.shape, block_rows.dtype),
            pltpu.VMEM((3, lines, LANES), jnp.float32),
            pltpu.VMEM(epsilon.shape, epsilon.dtype),
            pltpu.VMEM(factor.shape, factor.dtype),
            pltpu.VMEM((panels, per_column, HEAD * ROWS, tile), factor.dtype),
            *[pltpu.VMEM((slots,) + piece, jnp.float32) for slots in most + most],
            pltpu.VMEM(piece, jnp.float32),
            pltpu.VMEM((reals, lines, LANES), jnp.float32),
            pltpu.VMEM((3, sites, LANES), jnp.float32),
            pltpu.VMEM((sites, LANES), jnp.float32),
            pltpu.SMEM((2 * panels, SITE_TILES), jnp.int32),
            pltpu.SemaphoreType.DMA((1 + 2 * panels,)),
            pltpu.SemaphoreType.DMA((4,)),
            *[pltpu.SemaphoreType.DMA((slots,)) for slots in most + most],
            pltpu.SemaphoreType.DMA((reals,)),
            pltpu.SemaphoreType.DMA((reals,)),
        ],
        compiler_params=pltpu.CompilerParams(
            collective_id=0, has_side_effects=True, vmem_limit_bytes=60 * 1024 * 1024
        ),
    )(
        block_rows,
        epsilon,
        factor,
        median_log.reshape(lines, LANES),
        spread_log.reshape(lines, LANES),
        critical_yield.reshape(lines, LANES),
    )
    field, mean = pl.pallas_call(
        hand_out_kernel,
        out_shape=(
            jax.ShapeDtypeStruct(field.shape, field.dtype),
            jax.ShapeDtypeStruct(mean.shape, mean.dtype),
        ),
        in_specs=[vmem, vmem],
        out_specs=(anywhere, anywhere),
        scratch_shapes=[pltpu.SemaphoreType.DMA((PARTS + 1,))],
    )(pltpu.with_memory_space_constraint(field, pltpu.VMEM), pltpu.with_memory_space_constraint(mean, pltpu.VMEM))
    return field, mean.reshape(sites)


def solution(mesh):
    body = line_shards if mesh.shape["site"] == BAND // 2 + PAIR else shards
    return jax.shard_map(
        body,
        mesh=mesh,
        in_specs=(
            P("site", "real"),
            P(None, "site", None, None),
            P(None, "site"),
            P("site"),
            P("site"),
            P("site"),
        ),
        out_specs=(P("site", "real"), P("site")),
        check_vma=False,
    )
```
